32 devices in a mesh: row: 4 (over y, x), col: 8 (over z, core).
Axes of the slice: x: 2, y: 2, z: 4, core: 2. Of those that a mesh axis runs over, the one named last changes fastest.
Arguments:
- source: float32 [96, 128, 128], P('row', 'col'), may hold values from -24 to 24
- coefficient: float32 [96, 128, 128], P('row', 'col'), may hold values from 0.5 to 8
Outputs:
- relaxed: float32 [96, 128, 128], P('row', 'col')
The draws below stay inside these ranges and needn't reach their ends.
All inputs are finite; a program needn't handle non-finite values.
Results may differ from the reference program's by a relative error of at most 0.000071.
Values sent between devices are 32-bit elements; how exact they have to be, the bound alone decides.
A program may use at most 64 MiB of HBM per device.

```python
import math
import jax
import jax.numpy as jnp
from jax import lax

NZ = 128
SWEEPS = 4
NR = 96
NC = 128
LR = 48
LC = 64
LZ = 64


def block_levels(own_key, shape, shards, low, high):
    def one(axis_at, blocks):
        steps = jax.random.uniform(jax.random.fold_in(jax.random.fold_in(own_key, 6), axis_at), (blocks,), jnp.float32, low / len(shards), high / len(shards))
        return jnp.repeat(jnp.exp(steps), shape[axis_at] // blocks).reshape((-1,) + (1,) * (len(shape) - axis_at - 1))

    gain = one(*shards[0])
    for cut in shards[1:]:
        gain = gain * one(*cut)
    return gain


def bell_draw(rng, dims, width, most, split=(), kind=jnp.bfloat16):
    factor_of = block_levels(rng, dims, split, -0.22, 0.18) if split else 1.0
    entries = jax.random.normal(rng, dims, jnp.float32) * width * factor_of
    return jnp.minimum(jnp.maximum(entries, -most), most).astype(kind)


def setup_inputs(seed: int = 0) -> dict:
    splits = jax.random.split(jax.random.key(seed), 3)
    source = bell_draw(splits[0], (NR, NC, NZ), 4.0, 24.0, ((0, 4), (1, 8)), jnp.float32)
    coefficient = jnp.clip(jnp.exp(math.log(8.0) - 2.7725887 * jax.random.uniform(splits[1], (NR, NC, NZ), jnp.float32) ** block_levels(splits[1], (NR, NC, NZ), ((0, 4), (1, 8)), -0.2, 0.2)), 0.5, 8.0)
    return dict(source=source, coefficient=coefficient)


DAMPING = 0.8
SCREEN_SHIFT = 0.02
HIGHEST = lax.Precision.HIGHEST


def sine_table(length):
    series = jnp.arange(length, dtype=jnp.int32) + 1
    phases = (series[:, None] * series[None, :]) % (2 * (length + 1))
    return jnp.sin(jnp.pi * phases.astype(jnp.float32) / (length + 1))


def eigenvalues(positions, length):
    angles = jnp.pi * (positions + 1).astype(jnp.float32) / (2 * (length + 1))
    return 4.0 * jnp.sin(angles) ** 2


def neighbour_image(wide_field, diagonal_total):
    zpadded = jnp.pad(wide_field, ((0, 0), (0, 0), (1, 1)))
    center = wide_field[1:-1, 1:-1, :]
    beside = wide_field[2:, 1:-1] + wide_field[:-2, 1:-1] + wide_field[1:-1, 2:] + wide_field[1:-1, :-2]
    beside = beside + zpadded[1:-1, 1:-1, 2:] + zpadded[1:-1, 1:-1, :-2]
    return center, diagonal_total * center - beside


def relax_once(wide_field, diagonal_total, source):
    center, applied = neighbour_image(wide_field, diagonal_total)
    return center + DAMPING * (source - applied) / diagonal_total


def widened(iterate):
    return jnp.pad(iterate, ((1, 1), (1, 1), (0, 0)))


def reference(source, coefficient):
    diagonal_total = 6.0 + coefficient
    iterate = jnp.zeros_like(source)
    for repeat in range(SWEEPS):
        iterate = relax_once(widened(iterate), diagonal_total, source)
    center, applied = neighbour_image(widened(iterate), diagonal_total)
    residual = source - applied
    coarse = residual.reshape(LR, 2, LC, 2, LZ, 2).sum(axis=(1, 3, 5)) * 0.5
    table_z = sine_table(LZ)
    table_r = sine_table(LR)
    table_c = sine_table(LC)
    section = jnp.einsum('abz,zk->abk', coarse, table_z, precision=HIGHEST)
    section = jnp.einsum('abk,aj->jbk', section, table_r, precision=HIGHEST)
    section = jnp.einsum('jbk,bm->jmk', section, table_c, precision=HIGHEST)
    normaliser = (LZ + 1.0) * (LR + 1.0) * (LC + 1.0) / 8.0
    lam_z = eigenvalues(jnp.arange(LZ, dtype=jnp.int32), LZ)
    lam_r = eigenvalues(jnp.arange(LR, dtype=jnp.int32), LR)
    lam_c = eigenvalues(jnp.arange(LC, dtype=jnp.int32), LC)
    denominator = (SCREEN_SHIFT + lam_z[None, None, :] + lam_r[:, None, None] + lam_c[None, :, None]) * normaliser
    scaled = section / denominator
    section = jnp.einsum('jmk,mb->jbk', scaled, table_c, precision=HIGHEST)
    section = jnp.einsum('jbk,ja->abk', section, table_r, precision=HIGHEST)
    correction = jnp.einsum('abk,kz->abz', section, table_z, precision=HIGHEST)
    fine_corr = jnp.broadcast_to(correction[:, None, :, None, :, None], (LR, 2, LC, 2, LZ, 2)).reshape(NR, NC, NZ)
    iterate = iterate + fine_corr
    for repeat in range(SWEEPS):
        iterate = relax_once(widened(iterate), diagonal_total, source)
    return iterate
```

```python
import jax
import jax.numpy as jnp
import numpy as np
from jax import lax
from jax.experimental import pallas as pl
from jax.experimental.pallas import tpu as pltpu
from jax.sharding import PartitionSpec as P

SWEEPS = 4


DAMPING = 0.8
SCREEN_SHIFT = 0.02
HIGHEST = lax.Precision.HIGHEST


def padded(block, sides, width):
    for axis, dim in sides:
        count = lax.axis_size(axis)
        forward = [(i, i + 1) for i in range(count - 1)]
        backward = [(target, source) for source, target in forward]
        low = lax.ppermute(
            lax.slice_in_dim(block, block.shape[dim] - width, None, axis=dim), axis, forward
        )
        high = lax.ppermute(lax.slice_in_dim(block, 0, width, axis=dim), axis, backward)
        block = jnp.concatenate([low, block, high], axis=dim)
    return block


def sine_table(length):
    series = jnp.arange(length, dtype=jnp.int32) + 1
    phases = series[:, None] * series[None, :] % (2 * (length + 1))
    return jnp.sin(jnp.pi * phases.astype(jnp.float32) / (length + 1))


def eigenvalues(positions, length):
    angles = jnp.pi * (positions + 1).astype(jnp.float32) / (2 * (length + 1))
    return 4.0 * jnp.sin(angles) ** 2


def neighbour_image(wide_field, diagonal_total):
    zpadded = jnp.pad(wide_field, ((0, 0), (0, 0), (1, 1)))
    center = wide_field[1:-1, 1:-1, :]
    beside = (
        wide_field[2:, 1:-1] + wide_field[:-2, 1:-1] + wide_field[1:-1, 2:] + wide_field[1:-1, :-2]
    )
    beside = beside + zpadded[1:-1, 1:-1, 2:] + zpadded[1:-1, 1:-1, :-2]
    return (center, diagonal_total * center - beside)


def relax_once(wide_field, diagonal_total, source):
    center, applied = neighbour_image(wide_field, diagonal_total)
    return center + DAMPING * (source - applied) / diagonal_total


def trim_rim(tensor, margin):
    return tensor[margin : tensor.shape[0] - margin, margin : tensor.shape[1] - margin]


def inside_table(row_cells, col_cells, margin):
    row_ids = (
        lax.axis_index("row") * row_cells
        - margin
        + jnp.arange(row_cells + 2 * margin, dtype=jnp.int32)
    )
    col_ids = (
        lax.axis_index("col") * col_cells
        - margin
        + jnp.arange(col_cells + 2 * margin, dtype=jnp.int32)
    )
    row_inside = (row_ids >= 0) & (row_ids < row_cells * lax.axis_size("row"))
    col_inside = (col_ids >= 0) & (col_ids < col_cells * lax.axis_size("col"))
    return (row_inside[:, None] & col_inside[None, :]).astype(jnp.float32)[:, :, None]


def coarse_solve(residual):
    row_cells, col_cells, z_cells = residual.shape
    coarse_rows = row_cells // 2
    coarse_cols = col_cells // 2
    coarse_z = z_cells // 2
    total_r = coarse_rows * lax.axis_size("row")
    total_c = coarse_cols * lax.axis_size("col")
    z_slab = coarse_z // lax.axis_size("row")
    r_slab = total_r // lax.axis_size("col")
    coarse = residual.reshape(coarse_rows, 2, coarse_cols, 2, coarse_z, 2).sum(axis=(1, 3, 5)) * 0.5
    table_z = sine_table(coarse_z)
    table_r = sine_table(total_r)
    table_c = sine_table(total_c)
    ordered = jnp.transpose(coarse, (2, 1, 0))
    along_z = jnp.dot(table_z, ordered.reshape(coarse_z, -1), precision=HIGHEST).reshape(
        coarse_z, coarse_cols, coarse_rows
    )
    row_lines = lax.all_to_all(along_z, "row", split_axis=0, concat_axis=2, tiled=True)
    along_r = jnp.einsum("zcr,kr->zkc", row_lines, table_r, precision=HIGHEST)
    col_lines = lax.all_to_all(along_r, "col", split_axis=1, concat_axis=2, tiled=True)
    spectrum = jnp.dot(col_lines.reshape(-1, total_c), table_c, precision=HIGHEST).reshape(
        z_slab, r_slab, total_c
    )
    normaliser = (coarse_z + 1.0) * (total_r + 1.0) * (total_c + 1.0) / 8.0
    lam_z = eigenvalues(
        lax.axis_index("row") * z_slab + jnp.arange(z_slab, dtype=jnp.int32), coarse_z
    )
    lam_r = eigenvalues(
        lax.axis_index("col") * r_slab + jnp.arange(r_slab, dtype=jnp.int32), total_r
    )
    lam_c = eigenvalues(jnp.arange(total_c, dtype=jnp.int32), total_c)
    denominator = (
        SCREEN_SHIFT + lam_z[:, None, None] + lam_r[None, :, None] + lam_c[None, None, :]
    ) * normaliser
    scaled = spectrum / denominator
    back_c = jnp.dot(scaled.reshape(-1, total_c), table_c, precision=HIGHEST).reshape(
        z_slab, r_slab, total_c
    )
    returned = lax.all_to_all(back_c, "col", split_axis=2, concat_axis=1, tiled=True)
    back_r = jnp.einsum("zkc,kr->zcr", returned, table_r, precision=HIGHEST)
    owned = lax.all_to_all(back_r, "row", split_axis=2, concat_axis=0, tiled=True)
    back_z = jnp.dot(table_z, owned.reshape(coarse_z, -1), precision=HIGHEST).reshape(
        coarse_z, coarse_cols, coarse_rows
    )
    correction = jnp.transpose(back_z, (2, 1, 0))
    return jnp.broadcast_to(
        correction[:, None, :, None, :, None], (coarse_rows, 2, coarse_cols, 2, coarse_z, 2)
    ).reshape(row_cells, col_cells, z_cells)


def local_general(source, coefficient):
    row_cells, col_cells, z_cells = source.shape
    diagonal_total = 6.0 + coefficient
    opening = DAMPING * source / diagonal_total
    wide_first, wide_source, wide_coef = (
        padded(opening, (("row", 0), ("col", 1)), SWEEPS),
        padded(source, (("row", 0), ("col", 1)), SWEEPS),
        padded(coefficient, (("row", 0), ("col", 1)), SWEEPS),
    )
    wide_diag = 6.0 + wide_coef
    inside = inside_table(row_cells, col_cells, SWEEPS)
    wide_iter = wide_first
    for repeat in range(1, SWEEPS):
        wide_iter = relax_once(
            wide_iter, trim_rim(wide_diag, repeat), trim_rim(wide_source, repeat)
        ) * trim_rim(inside, repeat)
    iterate, applied = neighbour_image(wide_iter, diagonal_total)
    residual = source - applied
    iterate = iterate + coarse_solve(residual)
    wide_iter = padded(iterate, (("row", 0), ("col", 1)), SWEEPS)
    for repeat in range(1, SWEEPS + 1):
        wide_iter = relax_once(
            wide_iter, trim_rim(wide_diag, repeat), trim_rim(wide_source, repeat)
        ) * trim_rim(inside, repeat)
    return wide_iter


MESH = pl.DeviceIdType.MESH
SUBLANES = 8


def plain_sine(length):
    series = np.arange(length) + 1
    phases = series[:, None] * series[None, :] % (2 * (length + 1))
    return np.sin(np.pi * phases / (length + 1))


def plain_eigen(length):
    return 4.0 * np.sin(np.pi * (np.arange(length) + 1) / (2 * (length + 1))) ** 2


def solve_tables(n_row, n_col, kept, coarse_rows, coarse_cols, coarse_z):
    blocks = n_col * kept
    total_r, total_c = n_row * coarse_rows, n_col * coarse_cols
    sine_z, sine_r, sine_c = plain_sine(coarse_z), plain_sine(total_r), plain_sine(total_c)
    table_z = np.repeat(sine_z, 2, axis=1)
    forward_r = np.zeros((total_r, n_row, blocks))
    forward_r[:, :, :coarse_rows] = sine_r.reshape(total_r, n_row, coarse_rows)
    window_r = np.zeros((n_row, blocks, total_r))
    margin = (blocks - coarse_rows) // 2
    for r in range(n_row):
        for a in range(blocks):
            at = coarse_rows * r - margin + a
            if 0 <= at < total_r:
                window_r[r, a] = sine_r[at]
    table_c = np.zeros((n_col, kept, coarse_cols, kept, total_c))
    for k in range(kept):
        table_c[:, k, :, k, :] = sine_c.reshape(n_col, coarse_cols, total_c)
    normaliser = (coarse_z + 1.0) * (total_r + 1.0) * (total_c + 1.0) / 8.0
    base = SCREEN_SHIFT + plain_eigen(total_r)[:, None] + np.tile(plain_eigen(total_c), kept)[None, :]
    lam_z = np.repeat(plain_eigen(coarse_z).reshape(n_row * n_col, 1, kept), total_c, axis=2)
    lanes = kept * total_c
    tables = (
        table_z,
        forward_r.reshape(total_r, n_row * blocks),
        window_r.reshape(n_row * blocks, total_r),
        table_c.reshape(lanes, lanes),
        base * 2.0 * normaliser,
        lam_z * 2.0 * normaliser,
    )
    return tuple(np.asarray(t, np.float32) for t in tables)


def block_transpose(x, width):
    rows, lanes = x.shape
    row = lax.broadcasted_iota(jnp.int32, x.shape, 0)
    group = lax.broadcasted_iota(jnp.int32, x.shape, 1) // width
    step = 1
    while step < rows:
        row_bit = (row & step) != 0
        group_bit = (group & step) != 0
        from_below = pltpu.roll(pltpu.roll(x, width * step, 1), rows - step, 0)
        from_above = pltpu.roll(pltpu.roll(x, lanes - width * step, 1), step, 0)
        x = jnp.where(row_bit == group_bit, x, jnp.where(group_bit, from_below, from_above))
        step *= 2
    return x


def exact_dot(a, b, contract):
    return lax.dot_general(
        a, b, (contract, ((), ())), precision=HIGHEST, preferred_element_type=jnp.float32
    )


def step_kernel(
    sizes,
    source,
    coefficient,
    table_z,
    forward_r,
    window_r,
    table_c,
    base,
    lam_z,
    out,
    wide_s,
    wide_c,
    weight,
    first,
    field_a,
    field_b,
    rows_sum,
    fine_corr,
    send_a,
    recv_a,
    send_b,
    recv_b,
    own_sem,
    halo_send,
    halo_recv,
    fwd_send,
    fwd_recv,
    back_send,
    back_recv,
    ready,
):
    n_row, n_col, kept = sizes
    row_cells, col_cells, z_cells = source.shape
    coarse_rows, coarse_cols = row_cells // 2, col_cells // 2
    blocks = n_col * kept
    devices = n_row * n_col
    halo_r, halo_c = (wide_s.shape[0] - row_cells) // 2, SUBLANES
    wide_cols = wide_s.shape[1]
    my_row, my_col = lax.axis_index("row"), lax.axis_index("col")
    me = my_row * n_col + my_col

    steps = [(dr, dc) for dr in (-1, 0, 1) for dc in (-1, 0, 1) if (dr, dc) != (0, 0)]

    def exists(dr, dc):
        r, c = my_row + dr, my_col + dc
        return (r >= 0) & (r < n_row) & (c >= 0) & (c < n_col)

    barrier = pltpu.get_barrier_semaphore()
    for d in range(1, n_row):
        pl.semaphore_signal(
            barrier, 1, device_id=(lax.rem(my_row + d, n_row), my_col), device_id_type=MESH
        )
    for d in range(1, n_col):
        pl.semaphore_signal(
            barrier, 1, device_id=(my_row, lax.rem(my_col + d, n_col)), device_id_type=MESH
        )
    greeted = n_row + n_col - 2
    for dr, dc in steps:
        if dr and dc:
            there = exists(dr, dc)

            @pl.when(there)
            def _():
                pl.semaphore_signal(
                    barrier, 1, device_id=(my_row + dr, my_col + dc), device_id_type=MESH
                )

            greeted = greeted + there.astype(jnp.int32)

    arrays = ((source, wide_s), (coefficient, wide_c))
    own = [
        pltpu.make_async_copy(
            here, wide.at[pl.ds(halo_r, row_cells), pl.ds(0, col_cells)], own_sem.at[n]
        )
        for n, (here, wide) in enumerate(arrays)
    ]
    for copy in own:
        copy.start()

    def landing(dr, dc):
        rows = {-1: (0, halo_r), 0: (halo_r, row_cells), 1: (halo_r + row_cells, halo_r)}[dr]
        cols = {
            -1: (col_cells + halo_c, halo_c),
            0: (0, col_cells),
            1: (col_cells, halo_c),
        }[dc]
        return pl.ds(*rows), pl.ds(*cols)

    def leaving(dr, dc):
        rows = {-1: (0, halo_r), 0: (0, row_cells), 1: (row_cells - halo_r, halo_r)}[dr]
        cols = {-1: (0, halo_c), 0: (0, col_cells), 1: (col_cells - halo_c, halo_c)}[dc]
        return pl.ds(*rows), pl.ds(*cols)

    def halo_copy(n, at):
        dr, dc = steps[at]
        here, wide = arrays[n]
        return pltpu.make_async_remote_copy(
            src_ref=here.at[leaving(dr, dc)],
            dst_ref=wide.at[landing(-dr, -dc)],
            send_sem=halo_send.at[n, at],
            recv_sem=halo_recv.at[n, at],
            device_id=(my_row + dr, my_col + dc),
            device_id_type=MESH,
        )

    pl.semaphore_wait(barrier, greeted)
    for at in range(len(steps)):

        @pl.when(exists(*steps[at]))
        def _():
            for n in range(2):
                halo_copy(n, at).start()

    for d in range(1, n_row):
        pl.semaphore_signal(
            ready, 1, device_id=(lax.rem(my_row + d, n_row), my_col), device_id_type=MESH
        )

    for at, (dr, dc) in enumerate(steps):

        @pl.when(jnp.logical_not(exists(dr, dc)))
        def _():
            rows, cols = landing(dr, dc)
            wide_s[rows, cols] = jnp.zeros((rows.size, cols.size, z_cells), jnp.float32)
            wide_c[rows, cols] = jnp.zeros((rows.size, cols.size, z_cells), jnp.float32)

    for copy in own:
        copy.wait()
    for at in range(len(steps)):
        @pl.when(exists(*steps[len(steps) - 1 - at]))
        def _():
            for n in range(2):
                halo_copy(n, at).wait_recv()

    wide_rows = wide_s.shape[0]
    col_at = lax.broadcasted_iota(jnp.int32, (wide_cols, z_cells), 0)
    z_at = lax.broadcasted_iota(jnp.int32, (wide_cols, z_cells), 1)
    col_at = my_col * col_cells + jnp.where(col_at >= col_cells + halo_c, col_at - wide_cols, col_at)
    col_inside = (col_at >= 0) & (col_at < n_col * col_cells)
    not_first = z_at > 0
    not_last = z_at < z_cells - 1

    @pl.loop(0, wide_rows)
    def _(i):
        at = my_row * row_cells + i - halo_r
        inside = (at >= 0) & (at < n_row * row_cells)
        scale = jnp.where(inside & col_inside, DAMPING / (6.0 + wide_c[i]), 0.0)
        weight[i] = scale
        start = scale * wide_s[i]
        first[i] = start
        field_a[i] = start

    def beside(above, here, below):
        cols = here.shape[0]
        low = jnp.where(not_first[:cols], pltpu.roll(here, 1, 1), 0.0)
        high = jnp.where(not_last[:cols], pltpu.roll(here, z_cells - 1, 1), 0.0)
        return (
            (above + below)
            + (pltpu.roll(here, 1, 0) + pltpu.roll(here, cols - 1, 0))
            + (low + high)
        )

    def sweep(old, new, low, high, chunk, shift=0, cols=wide_cols):
        @pl.loop(0, (high - low) // chunk)
        def _(n):
            i = low + n * chunk
            lines = [old[i - 1 + m] for m in range(chunk + 2)]
            for m in range(chunk):
                here = lines[m + 1]
                fresh = (1.0 - DAMPING) * here + (
                    first[i + m] + weight[i + m] * beside(lines[m], here, lines[m + 2])
                )
                new[i + m - shift] = fresh[:cols]

    fields = (field_a, field_b)
    for turn in range(1, SWEEPS):
        sweep(fields[(turn - 1) % 2], fields[turn % 2], 1, wide_rows - 1, 4)
    smooth, other = fields[(SWEEPS - 1) % 2], fields[SWEEPS % 2]

    @pl.loop(0, coarse_rows)
    def _(a):
        i = halo_r + 2 * a
        lines = [smooth[i - 1 + m] for m in range(4)]
        total = None
        for m in range(2):
            near = beside(lines[m], lines[m + 1], lines[m + 2])
            left = wide_s[i + m] + (near - (6.0 + wide_c[i + m]) * lines[m + 1])
            total = left if total is None else total + left
        rows_sum[a] = total[:col_cells]

    pairs = [
        rows_sum[a, pl.ds(0, coarse_cols, stride=2), :]
        + rows_sum[a, pl.ds(1, coarse_cols, stride=2), :]
        for a in range(coarse_rows)
    ]
    blank = jnp.zeros(((blocks - coarse_rows) * coarse_cols, z_cells), jnp.float32)
    along_z = exact_dot(
        table_z[...], jnp.concatenate(pairs + [blank], axis=0), ((1,), (1,))
    )
    for q in range(devices):
        send_a[q] = along_z[q * kept : (q + 1) * kept]

    pl.semaphore_wait(ready, n_row - 1)

    def exchange(send, recv, send_sem, recv_sem):
        def copy(d):
            target = lax.rem(me + d, devices)
            return pltpu.make_async_remote_copy(
                src_ref=send.at[target],
                dst_ref=recv.at[me],
                send_sem=send_sem.at[d],
                recv_sem=recv_sem.at[d],
                device_id=(lax.div(target, n_col), lax.rem(target, n_col)),
                device_id_type=MESH,
            )

        @pl.loop(1, devices)
        def _(d):
            copy(d).start()

        recv[me] = send[me]

        @pl.loop(1, devices)
        def _(d):
            copy(d).wait_recv()

        return copy

    forward = exchange(send_a, recv_a, fwd_send, fwd_recv)

    gathered = jnp.concatenate(
        [
            block_transpose(
                recv_a[pl.ds(r * n_col, n_col)].reshape(blocks, z_cells), coarse_cols
            )
            for r in range(n_row)
        ],
        axis=0,
    )
    along_r = exact_dot(forward_r[...], gathered, ((1,), (0,)))
    spectrum = exact_dot(along_r, table_c[...], ((1,), (0,)))
    scaled = spectrum / (base[...] + lam_z[me])
    back_c = exact_dot(scaled, table_c[...], ((1,), (1,)))
    back_r = exact_dot(window_r[...], back_c, ((1,), (0,)))
    lane = lax.broadcasted_iota(jnp.int32, (blocks, z_cells), 1)
    column = lane // (kept * coarse_cols)
    late = lane % coarse_cols >= coarse_cols // 2
    for r in range(n_row):
        plane = back_r[r * blocks : (r + 1) * blocks]
        right = jnp.where(
            column < n_col - 1, pltpu.roll(plane, z_cells - kept * coarse_cols, 1), 0.0
        )
        left = jnp.where(column > 0, pltpu.roll(plane, kept * coarse_cols, 1), 0.0)
        at = pl.ds(r * n_col, n_col)
        send_b[at, pl.ds(0, kept)] = block_transpose(plane, coarse_cols).reshape(
            n_col, kept, z_cells
        )
        send_b[at, pl.ds(kept, kept)] = block_transpose(
            jnp.where(late, left, right), coarse_cols
        ).reshape(n_col, kept, z_cells)

    backward = exchange(send_b, recv_b, back_send, back_recv)

    modes = devices * kept
    for part in range(2):
        lines = recv_b[:, pl.ds(part * kept, kept)].reshape(modes, z_cells)
        values = exact_dot(jnp.transpose(lines), table_z[...], ((1,), (0,)))
        for a in range(blocks):
            for odd in range(2):
                fine_corr[a, pl.ds(part * col_cells + odd, coarse_cols, stride=2), :] = values[
                    a * coarse_cols : (a + 1) * coarse_cols
                ]

    margin = halo_r - (blocks - coarse_rows)

    @pl.loop(0, blocks)
    def _(a):
        i = margin + 2 * a
        smooth[i] = smooth[i] + fine_corr[a]
        smooth[i + 1] = smooth[i + 1] + fine_corr[a]

    fields = (smooth, other)
    for turn in range(SWEEPS):
        low, high = margin + 1 + turn, wide_rows - margin - 1 - turn
        if turn < SWEEPS - 1:
            sweep(fields[turn % 2], fields[(turn + 1) % 2], low, high, 2)
        else:
            sweep(fields[turn % 2], out, low, high, 2, low, col_cells)

    for at in range(len(steps)):

        @pl.when(exists(*steps[at]))
        def _():
            for n in range(2):
                halo_copy(n, at).wait_send()

    @pl.loop(1, devices)
    def _(d):
        forward(d).wait_send()
        backward(d).wait_send()


def local_kernel(n_row, n_col, source, coefficient):
    row_cells, col_cells, z_cells = source.shape
    coarse_rows, coarse_cols, coarse_z = row_cells // 2, col_cells // 2, z_cells // 2
    devices = n_row * n_col
    kept = coarse_z // devices
    blocks = n_col * kept
    tables = solve_tables(n_row, n_col, kept, coarse_rows, coarse_cols, coarse_z)
    wide = (row_cells + 2 * (2 * SWEEPS - 1), col_cells + 2 * SUBLANES, z_cells)
    dma = pltpu.SemaphoreType.DMA
    f32 = jnp.float32

    def body(*refs):
        step_kernel((n_row, n_col, kept), *refs)

    return pl.pallas_call(
        body,
        out_shape=jax.ShapeDtypeStruct(source.shape, f32),
        in_specs=[pl.BlockSpec(memory_space=pl.ANY)] * 2
        + [pl.BlockSpec(memory_space=pltpu.VMEM)] * len(tables),
        out_specs=pl.BlockSpec(memory_space=pltpu.VMEM),
        scratch_shapes=[pltpu.VMEM(wide, f32)] * 6
        + [
            pltpu.VMEM((coarse_rows, col_cells, z_cells), f32),
            pltpu.VMEM((blocks, 2 * col_cells, z_cells), f32),
            pltpu.VMEM((devices, kept, z_cells), f32),
            pltpu.VMEM((devices, kept, z_cells), f32),
            pltpu.VMEM((devices, 2 * kept, z_cells), f32),
            pltpu.VMEM((devices, 2 * kept, z_cells), f32),
            dma((2,)),
            dma((2, 8)),
            dma((2, 8)),
            dma((devices,)),
            dma((devices,)),
            dma((devices,)),
            dma((devices,)),
            pltpu.SemaphoreType.REGULAR,
        ],
        compiler_params=pltpu.CompilerParams(collective_id=0, has_side_effects=True),
        name="vstep",
    )(source, coefficient, *(jnp.asarray(t) for t in tables))


def fits_kernel(n_row, n_col, source):
    row_cells, col_cells, z_cells = source.shape
    devices = n_row * n_col
    kept = (z_cells // 2) // devices
    blocks = n_col * kept
    return (
        kept * devices * 2 == z_cells
        and z_cells == 128
        and col_cells == 2 * SUBLANES
        and blocks * (col_cells // 2) == z_cells
        and blocks == row_cells // 2 + SWEEPS
        and row_cells >= 2 * SWEEPS - 1
    )


def solution(mesh):
    n_row, n_col = mesh.shape["row"], mesh.shape["col"]

    def local(source, coefficient):
        if fits_kernel(n_row, n_col, source):
            return local_kernel(n_row, n_col, source, coefficient)
        return local_general(source, coefficient)

    return jax.shard_map(
        local,
        mesh=mesh,
        in_specs=(P("row", "col", None), P("row", "col", None)),
        out_specs=P("row", "col", None),
        check_vma=False,
    )
```

```python
import jax
import jax.numpy as jnp
import numpy as np
from jax import lax
from jax.experimental import pallas as pl
from jax.experimental.pallas import tpu as pltpu
from jax.sharding import PartitionSpec as P

SWEEPS = 4


DAMPING = 0.8
SCREEN_SHIFT = 0.02
HIGHEST = lax.Precision.HIGHEST


def padded(block, sides, width):
    for axis, dim in sides:
        count = lax.axis_size(axis)
        forward = [(i, i + 1) for i in range(count - 1)]
        backward = [(target, source) for source, target in forward]
        low = lax.ppermute(
            lax.slice_in_dim(block, block.shape[dim] - width, None, axis=dim), axis, forward
        )
        high = lax.ppermute(lax.slice_in_dim(block, 0, width, axis=dim), axis, backward)
        block = jnp.concatenate([low, block, high], axis=dim)
    return block


def sine_table(length):
    series = jnp.arange(length, dtype=jnp.int32) + 1
    phases = series[:, None] * series[None, :] % (2 * (length + 1))
    return jnp.sin(jnp.pi * phases.astype(jnp.float32) / (length + 1))


def eigenvalues(positions, length):
    angles = jnp.pi * (positions + 1).astype(jnp.float32) / (2 * (length + 1))
    return 4.0 * jnp.sin(angles) ** 2


def neighbour_image(wide_field, diagonal_total):
    zpadded = jnp.pad(wide_field, ((0, 0), (0, 0), (1, 1)))
    center = wide_field[1:-1, 1:-1, :]
    beside = (
        wide_field[2:, 1:-1] + wide_field[:-2, 1:-1] + wide_field[1:-1, 2:] + wide_field[1:-1, :-2]
    )
    beside = beside + zpadded[1:-1, 1:-1, 2:] + zpadded[1:-1, 1:-1, :-2]
    return (center, diagonal_total * center - beside)


def relax_once(wide_field, diagonal_total, source):
    center, applied = neighbour_image(wide_field, diagonal_total)
    return center + DAMPING * (source - applied) / diagonal_total


def trim_rim(tensor, margin):
    return tensor[margin : tensor.shape[0] - margin, margin : tensor.shape[1] - margin]


def inside_table(row_cells, col_cells, margin):
    row_ids = (
        lax.axis_index("row") * row_cells
        - margin
        + jnp.arange(row_cells + 2 * margin, dtype=jnp.int32)
    )
    col_ids = (
        lax.axis_index("col") * col_cells
        - margin
        + jnp.arange(col_cells + 2 * margin, dtype=jnp.int32)
    )
    row_inside = (row_ids >= 0) & (row_ids < row_cells * lax.axis_size("row"))
    col_inside = (col_ids >= 0) & (col_ids < col_cells * lax.axis_size("col"))
    return (row_inside[:, None] & col_inside[None, :]).astype(jnp.float32)[:, :, None]


def coarse_solve(residual):
    row_cells, col_cells, z_cells = residual.shape
    coarse_rows = row_cells // 2
    coarse_cols = col_cells // 2
    coarse_z = z_cells // 2
    total_r = coarse_rows * lax.axis_size("row")
    total_c = coarse_cols * lax.axis_size("col")
    z_slab = coarse_z // lax.axis_size("row")
    r_slab = total_r // lax.axis_size("col")
    coarse = residual.reshape(coarse_rows, 2, coarse_cols, 2, coarse_z, 2).sum(axis=(1, 3, 5)) * 0.5
    table_z = sine_table(coarse_z)
    table_r = sine_table(total_r)
    table_c = sine_table(total_c)
    ordered = jnp.transpose(coarse, (2, 1, 0))
    along_z = jnp.dot(table_z, ordered.reshape(coarse_z, -1), precision=HIGHEST).reshape(
        coarse_z, coarse_cols, coarse_rows
    )
    row_lines = lax.all_to_all(along_z, "row", split_axis=0, concat_axis=2, tiled=True)
    along_r = jnp.einsum("zcr,kr->zkc", row_lines, table_r, precision=HIGHEST)
    col_lines = lax.all_to_all(along_r, "col", split_axis=1, concat_axis=2, tiled=True)
    spectrum = jnp.dot(col_lines.reshape(-1, total_c), table_c, precision=HIGHEST).reshape(
        z_slab, r_slab, total_c
    )
    normaliser = (coarse_z + 1.0) * (total_r + 1.0) * (total_c + 1.0) / 8.0
    lam_z = eigenvalues(
        lax.axis_index("row") * z_slab + jnp.arange(z_slab, dtype=jnp.int32), coarse_z
    )
    lam_r = eigenvalues(
        lax.axis_index("col") * r_slab + jnp.arange(r_slab, dtype=jnp.int32), total_r
    )
    lam_c = eigenvalues(jnp.arange(total_c, dtype=jnp.int32), total_c)
    denominator = (
        SCREEN_SHIFT + lam_z[:, None, None] + lam_r[None, :, None] + lam_c[None, None, :]
    ) * normaliser
    scaled = spectrum / denominator
    back_c = jnp.dot(scaled.reshape(-1, total_c), table_c, precision=HIGHEST).reshape(
        z_slab, r_slab, total_c
    )
    returned = lax.all_to_all(back_c, "col", split_axis=2, concat_axis=1, tiled=True)
    back_r = jnp.einsum("zkc,kr->zcr", returned, table_r, precision=HIGHEST)
    owned = lax.all_to_all(back_r, "row", split_axis=2, concat_axis=0, tiled=True)
    back_z = jnp.dot(table_z, owned.reshape(coarse_z, -1), precision=HIGHEST).reshape(
        coarse_z, coarse_cols, coarse_rows
    )
    correction = jnp.transpose(back_z, (2, 1, 0))
    return jnp.broadcast_to(
        correction[:, None, :, None, :, None], (coarse_rows, 2, coarse_cols, 2, coarse_z, 2)
    ).reshape(row_cells, col_cells, z_cells)


def local_general(source, coefficient):
    row_cells, col_cells, z_cells = source.shape
    diagonal_total = 6.0 + coefficient
    opening = DAMPING * source / diagonal_total
    wide_first, wide_source, wide_coef = (
        padded(opening, (("row", 0), ("col", 1)), SWEEPS),
        padded(source, (("row", 0), ("col", 1)), SWEEPS),
        padded(coefficient, (("row", 0), ("col", 1)), SWEEPS),
    )
    wide_diag = 6.0 + wide_coef
    inside = inside_table(row_cells, col_cells, SWEEPS)
    wide_iter = wide_first
    for repeat in range(1, SWEEPS):
        wide_iter = relax_once(
            wide_iter, trim_rim(wide_diag, repeat), trim_rim(wide_source, repeat)
        ) * trim_rim(inside, repeat)
    iterate, applied = neighbour_image(wide_iter, diagonal_total)
    residual = source - applied
    iterate = iterate + coarse_solve(residual)
    wide_iter = padded(iterate, (("row", 0), ("col", 1)), SWEEPS)
    for repeat in range(1, SWEEPS + 1):
        wide_iter = relax_once(
            wide_iter, trim_rim(wide_diag, repeat), trim_rim(wide_source, repeat)
        ) * trim_rim(inside, repeat)
    return wide_iter


MESH = pl.DeviceIdType.MESH
SUBLANES = 8
MOST_ROWS = 15


def plain_sine(length):
    series = np.arange(length) + 1
    phases = series[:, None] * series[None, :] % (2 * (length + 1))
    return np.sin(np.pi * phases / (length + 1))


def plain_eigen(length):
    return 4.0 * np.sin(np.pi * (np.arange(length) + 1) / (2 * (length + 1))) ** 2


def solve_tables(n_row, n_col, kept, coarse_rows, coarse_cols, coarse_z):
    blocks = n_col * kept
    total_r, total_c = n_row * coarse_rows, n_col * coarse_cols
    sine_z, sine_r, sine_c = plain_sine(coarse_z), plain_sine(total_r), plain_sine(total_c)
    table_z = np.repeat(sine_z, 2, axis=1)
    forward_r = np.zeros((total_r, n_row, blocks))
    forward_r[:, :, :coarse_rows] = sine_r.reshape(total_r, n_row, coarse_rows)
    window_r = np.zeros((n_row, blocks, total_r))
    margin = (blocks - coarse_rows) // 2
    for r in range(n_row):
        for a in range(blocks):
            at = coarse_rows * r - margin + a
            if 0 <= at < total_r:
                window_r[r, a] = sine_r[at]
    table_c = np.zeros((n_col, kept, coarse_cols, kept, total_c))
    for k in range(kept):
        table_c[:, k, :, k, :] = sine_c.reshape(n_col, coarse_cols, total_c)
    normaliser = (coarse_z + 1.0) * (total_r + 1.0) * (total_c + 1.0) / 8.0
    base = SCREEN_SHIFT + plain_eigen(total_r)[:, None] + np.tile(plain_eigen(total_c), kept)[None, :]
    lam_z = np.repeat(plain_eigen(coarse_z).reshape(n_row * n_col, 1, kept), total_c, axis=2)
    lanes = kept * total_c
    tables = (
        table_z,
        forward_r.reshape(total_r, n_row * blocks),
        window_r.reshape(n_row * blocks, total_r),
        table_c.reshape(lanes, lanes),
        base * 2.0 * normaliser,
        lam_z * 2.0 * normaliser,
    )
    return tuple(np.asarray(t, np.float32) for t in tables)


def block_transpose(x, width):
    rows, lanes = x.shape
    row = lax.broadcasted_iota(jnp.int32, x.shape, 0)
    group = lax.broadcasted_iota(jnp.int32, x.shape, 1) // width
    step = 1
    while step < rows:
        row_bit = (row & step) != 0
        group_bit = (group & step) != 0
        from_below = pltpu.roll(pltpu.roll(x, width * step, 1), rows - step, 0)
        from_above = pltpu.roll(pltpu.roll(x, lanes - width * step, 1), step, 0)
        x = jnp.where(row_bit == group_bit, x, jnp.where(group_bit, from_below, from_above))
        step *= 2
    return x


def exact_dot(a, b, contract):
    return lax.dot_general(
        a, b, (contract, ((), ())), precision=HIGHEST, preferred_element_type=jnp.float32
    )


def step_kernel(
    sizes,
    source,
    coefficient,
    table_z_in,
    forward_r_in,
    window_r_in,
    table_c_in,
    base_in,
    lam_z_in,
    out,
    table_z,
    forward_r,
    window_r,
    table_c,
    base,
    lam_z,
    wide_s,
    wide_c,
    weight,
    first,
    field_a,
    field_b,
    rows_sum,
    fine_corr,
    send_a,
    recv_a,
    send_b,
    recv_b,
    own_sem,
    table_sem,
    halo_send,
    halo_recv,
    fwd_send,
    fwd_recv,
    back_send,
    back_recv,
    ready,
):
    n_row, n_col, kept = sizes
    row_cells, col_cells, z_cells = source.shape
    coarse_rows, coarse_cols = row_cells // 2, col_cells // 2
    blocks = n_col * kept
    devices = n_row * n_col
    halo_r, halo_c = (wide_s.shape[0] - row_cells) // 2, SUBLANES
    wide_cols = wide_s.shape[1]
    my_row, my_col = lax.axis_index("row"), lax.axis_index("col")
    me = my_row * n_col + my_col

    steps = [(dr, dc) for dr in (-1, 0, 1) for dc in (-1, 0, 1) if (dr, dc) != (0, 0)]

    def exists(dr, dc):
        r, c = my_row + dr, my_col + dc
        return (r >= 0) & (r < n_row) & (c >= 0) & (c < n_col)

    barrier = pltpu.get_barrier_semaphore()
    for d in range(1, n_row):
        pl.semaphore_signal(
            barrier, 1, device_id=(lax.rem(my_row + d, n_row), my_col), device_id_type=MESH
        )
    for d in range(1, n_col):
        pl.semaphore_signal(
            barrier, 1, device_id=(my_row, lax.rem(my_col + d, n_col)), device_id_type=MESH
        )
    greeted = n_row + n_col - 2
    for dr, dc in steps:
        if dr and dc:
            there = exists(dr, dc)

            @pl.when(there)
            def _():
                pl.semaphore_signal(
                    barrier, 1, device_id=(my_row + dr, my_col + dc), device_id_type=MESH
                )

            greeted = greeted + there.astype(jnp.int32)

    arrays = ((source, wide_s), (coefficient, wide_c))
    own = [
        pltpu.make_async_copy(
            here, wide.at[pl.ds(halo_r, row_cells), pl.ds(0, col_cells)], own_sem.at[n]
        )
        for n, (here, wide) in enumerate(arrays)
    ]
    for copy in own:
        copy.start()
    staged = [
        pltpu.make_async_copy(given, held, table_sem.at[n])
        for n, (given, held) in enumerate(
            (
                (table_z_in, table_z),
                (forward_r_in, forward_r),
                (window_r_in, window_r),
                (table_c_in, table_c),
                (base_in, base),
                (lam_z_in, lam_z),
            )
        )
    ]
    for copy in staged:
        copy.start()

    near_r = SWEEPS
    far_r = halo_r - near_r
    portions = (steps, [step for step in steps if step[0]])

    def landing(far, dr, dc):
        if far:
            rows = {-1: (0, far_r), 1: (halo_r + row_cells + near_r, far_r)}[dr]
        else:
            rows = {
                -1: (far_r, near_r),
                0: (halo_r, row_cells),
                1: (halo_r + row_cells, near_r),
            }[dr]
        cols = {
            -1: (col_cells + halo_c, halo_c),
            0: (0, col_cells),
            1: (col_cells, halo_c),
        }[dc]
        return pl.ds(*rows), pl.ds(*cols)

    def leaving(far, dr, dc):
        if far:
            rows = {-1: (near_r, far_r), 1: (row_cells - halo_r, far_r)}[dr]
        else:
            rows = {-1: (0, near_r), 0: (0, row_cells), 1: (row_cells - near_r, near_r)}[dr]
        cols = {-1: (0, halo_c), 0: (0, col_cells), 1: (col_cells - halo_c, halo_c)}[dc]
        return pl.ds(*rows), pl.ds(*cols)

    def halo_copies(far, dr, dc):
        at = steps.index((dr, dc))
        return [
            pltpu.make_async_remote_copy(
                src_ref=here.at[leaving(far, dr, dc)],
                dst_ref=wide.at[landing(far, -dr, -dc)],
                send_sem=halo_send.at[far, n, at],
                recv_sem=halo_recv.at[far, n, at],
                device_id=(my_row + dr, my_col + dc),
                device_id_type=MESH,
            )
            for n, (here, wide) in enumerate(arrays)
        ]

    def start_halo(far):
        for step in portions[far]:

            @pl.when(exists(*step))
            def _():
                for copy in halo_copies(far, *step):
                    copy.start()

    def fill_halo(far):
        for step in portions[far]:

            @pl.when(jnp.logical_not(exists(*step)))
            def _():
                rows, cols = landing(far, *step)
                for _, wide in arrays:
                    wide[rows, cols] = jnp.zeros((rows.size, cols.size, z_cells), jnp.float32)

    def wait_halo(far):
        for dr, dc in portions[far]:
            @pl.when(exists(-dr, -dc))
            def _():
                for copy in halo_copies(far, dr, dc):
                    copy.wait_recv()

    pl.semaphore_wait(barrier, greeted)
    start_halo(0)
    for d in range(1, n_row):
        pl.semaphore_signal(
            ready, 1, device_id=(lax.rem(my_row + d, n_row), my_col), device_id_type=MESH
        )
    start_halo(1)
    fill_halo(0)
    fill_halo(1)
    for copy in own:
        copy.wait()
    wait_halo(0)

    wide_rows = wide_s.shape[0]
    col_at = lax.broadcasted_iota(jnp.int32, (wide_cols, z_cells), 0)
    z_at = lax.broadcasted_iota(jnp.int32, (wide_cols, z_cells), 1)
    col_at = my_col * col_cells + jnp.where(col_at >= col_cells + halo_c, col_at - wide_cols, col_at)
    col_inside = (col_at >= 0) & (col_at < n_col * col_cells)
    not_first = z_at > 0
    not_last = z_at < z_cells - 1

    def prepare(i):
        at = my_row * row_cells + i - halo_r
        inside = (at >= 0) & (at < n_row * row_cells)
        scale = jnp.where(inside & col_inside, DAMPING / (6.0 + wide_c[i]), 0.0)
        weight[i] = scale
        first[i] = scale * wide_s[i]

    piece = SUBLANES // 2

    @pl.loop(0, (row_cells + 2 * near_r) // piece)
    def _(n):
        for m in range(piece):
            prepare(far_r + n * piece + m)

    def beside(above, here, below):
        cols = here.shape[0]
        low = jnp.where(not_first[:cols], pltpu.roll(here, 1, 1), 0.0)
        high = jnp.where(not_last[:cols], pltpu.roll(here, z_cells - 1, 1), 0.0)
        return (
            (above + below)
            + (pltpu.roll(here, 1, 0) + pltpu.roll(here, cols - 1, 0))
            + (low + high)
        )

    def sweep(old, new, low, high, shift=0, cols=wide_cols):
        chunk = max(m for m in range(1, MOST_ROWS + 1) if (high - low) % m == 0)

        def work(i):
            lines = [old[i - 1 + m] for m in range(chunk + 2)]
            for m in range(chunk):
                here = lines[m + 1]
                fresh = (1.0 - DAMPING) * here + (
                    first[i + m] + weight[i + m] * beside(lines[m], here, lines[m + 2])
                )
                new[i + m - shift] = fresh[:cols]

        if chunk == high - low:
            work(low)
        else:

            @pl.loop(0, (high - low) // chunk)
            def _(n):
                work(low + n * chunk)

    fields = (first,) + (field_b, field_a) * SWEEPS
    smooth, other = fields[SWEEPS - 1], fields[SWEEPS]
    for turn in range(1, SWEEPS):
        sweep(fields[turn - 1], fields[turn], far_r + turn, wide_rows - far_r - turn)

    def widen():
        wait_halo(1)
        for i in range(far_r):
            prepare(i)
            prepare(wide_rows - 1 - i)
        for turn in range(1, SWEEPS):
            sweep(fields[turn - 1], fields[turn], turn, far_r + turn)
            sweep(
                fields[turn - 1], fields[turn], wide_rows - far_r - turn, wide_rows - turn
            )

    @pl.loop(0, coarse_rows)
    def _(a):
        i = halo_r + 2 * a
        lines = [smooth[i - 1 + m] for m in range(4)]
        total = None
        for m in range(2):
            near = beside(lines[m], lines[m + 1], lines[m + 2])
            left = wide_s[i + m] + (near - (6.0 + wide_c[i + m]) * lines[m + 1])
            total = left if total is None else total + left
        rows_sum[a] = total[:col_cells]

    for copy in staged:
        copy.wait()
    pairs = [
        rows_sum[a, pl.ds(0, coarse_cols, stride=2), :]
        + rows_sum[a, pl.ds(1, coarse_cols, stride=2), :]
        for a in range(coarse_rows)
    ]
    blank = jnp.zeros(((blocks - coarse_rows) * coarse_cols, z_cells), jnp.float32)
    along_z = exact_dot(
        table_z[...], jnp.concatenate(pairs + [blank], axis=0), ((1,), (1,))
    )
    for q in range(devices):
        send_a[q] = along_z[q * kept : (q + 1) * kept]

    pl.semaphore_wait(ready, n_row - 1)

    def exchange(send, recv, send_sem, recv_sem, meanwhile=None):
        def copy(d):
            target = lax.rem(me + d, devices)
            return pltpu.make_async_remote_copy(
                src_ref=send.at[target],
                dst_ref=recv.at[me],
                send_sem=send_sem.at[d],
                recv_sem=recv_sem.at[d],
                device_id=(lax.div(target, n_col), lax.rem(target, n_col)),
                device_id_type=MESH,
            )

        @pl.loop(1, devices)
        def _(d):
            copy(d).start()

        recv[me] = send[me]
        if meanwhile is not None:
            meanwhile()

        @pl.loop(1, devices)
        def _(d):
            copy(d).wait_recv()

        return copy

    forward = exchange(send_a, recv_a, fwd_send, fwd_recv, widen)

    gathered = jnp.concatenate(
        [
            block_transpose(
                recv_a[pl.ds(r * n_col, n_col)].reshape(blocks, z_cells), coarse_cols
            )
            for r in range(n_row)
        ],
        axis=0,
    )
    along_r = exact_dot(forward_r[...], gathered, ((1,), (0,)))
    spectrum = exact_dot(along_r, table_c[...], ((1,), (0,)))
    scaled = spectrum / (base[...] + lam_z[me])
    back_c = exact_dot(scaled, table_c[...], ((1,), (1,)))
    back_r = exact_dot(window_r[...], back_c, ((1,), (0,)))
    lane = lax.broadcasted_iota(jnp.int32, (blocks, z_cells), 1)
    column = lane // (kept * coarse_cols)
    late = lane % coarse_cols >= coarse_cols // 2
    for r in range(n_row):
        plane = back_r[r * blocks : (r + 1) * blocks]
        right = jnp.where(
            column < n_col - 1, pltpu.roll(plane, z_cells - kept * coarse_cols, 1), 0.0
        )
        left = jnp.where(column > 0, pltpu.roll(plane, kept * coarse_cols, 1), 0.0)
        at = pl.ds(r * n_col, n_col)
        send_b[at, pl.ds(0, kept)] = block_transpose(plane, coarse_cols).reshape(
            n_col, kept, z_cells
        )
        send_b[at, pl.ds(kept, kept)] = block_transpose(
            jnp.where(late, left, right), coarse_cols
        ).reshape(n_col, kept, z_cells)

    backward = exchange(send_b, recv_b, back_send, back_recv)

    modes = devices * kept
    for part in range(2):
        lines = recv_b[:, pl.ds(part * kept, kept)].reshape(modes, z_cells)
        values = exact_dot(jnp.transpose(lines), table_z[...], ((1,), (0,)))
        for a in range(blocks):
            for odd in range(2):
                fine_corr[a, pl.ds(part * col_cells + odd, coarse_cols, stride=2), :] = values[
                    a * coarse_cols : (a + 1) * coarse_cols
                ]

    margin = halo_r - (blocks - coarse_rows)

    @pl.loop(0, blocks)
    def _(a):
        i = margin + 2 * a
        smooth[i] = smooth[i] + fine_corr[a]
        smooth[i + 1] = smooth[i + 1] + fine_corr[a]

    fields = (smooth, other) * SWEEPS
    for turn in range(SWEEPS):
        low, high = margin + 1 + turn, wide_rows - margin - 1 - turn
        if turn < SWEEPS - 1:
            sweep(fields[turn], fields[turn + 1], low, high)
        else:
            sweep(fields[turn], out, low, high, low, col_cells)

    for far in range(2):
        for step in portions[far]:

            @pl.when(exists(*step))
            def _():
                for copy in halo_copies(far, *step):
                    copy.wait_send()

    @pl.loop(1, devices)
    def _(d):
        forward(d).wait_send()
        backward(d).wait_send()


def local_kernel(n_row, n_col, source, coefficient):
    row_cells, col_cells, z_cells = source.shape
    coarse_rows, coarse_cols, coarse_z = row_cells // 2, col_cells // 2, z_cells // 2
    devices = n_row * n_col
    kept = coarse_z // devices
    blocks = n_col * kept
    tables = solve_tables(n_row, n_col, kept, coarse_rows, coarse_cols, coarse_z)
    wide = (row_cells + 2 * (2 * SWEEPS - 1), col_cells + 2 * SUBLANES, z_cells)
    dma = pltpu.SemaphoreType.DMA
    f32 = jnp.float32

    def body(*refs):
        step_kernel((n_row, n_col, kept), *refs)

    return pl.pallas_call(
        body,
        out_shape=jax.ShapeDtypeStruct(source.shape, f32),
        in_specs=[pl.BlockSpec(memory_space=pl.ANY)] * (2 + len(tables)),
        out_specs=pl.BlockSpec(memory_space=pltpu.VMEM),
        scratch_shapes=[pltpu.VMEM(t.shape, f32) for t in tables]
        + [pltpu.VMEM(wide, f32)] * 6
        + [
            pltpu.VMEM((coarse_rows, col_cells, z_cells), f32),
            pltpu.VMEM((blocks, 2 * col_cells, z_cells), f32),
            pltpu.VMEM((devices, kept, z_cells), f32),
            pltpu.VMEM((devices, kept, z_cells), f32),
            pltpu.VMEM((devices, 2 * kept, z_cells), f32),
            pltpu.VMEM((devices, 2 * kept, z_cells), f32),
            dma((2,)),
            dma((len(tables),)),
            dma((2, 2, 8)),
            dma((2, 2, 8)),
            dma((devices,)),
            dma((devices,)),
            dma((devices,)),
            dma((devices,)),
            pltpu.SemaphoreType.REGULAR,
        ],
        compiler_params=pltpu.CompilerParams(collective_id=0, has_side_effects=True),
        name="vstep",
    )(source, coefficient, *(jnp.asarray(t) for t in tables))


def fits_kernel(n_row, n_col, source):
    row_cells, col_cells, z_cells = source.shape
    devices = n_row * n_col
    kept = (z_cells // 2) // devices
    blocks = n_col * kept
    return (
        kept * devices * 2 == z_cells
        and z_cells == 128
        and col_cells == 2 * SUBLANES
        and blocks * (col_cells // 2) == z_cells
        and blocks == row_cells // 2 + SWEEPS
        and row_cells >= 2 * SWEEPS - 1
        and (row_cells + 2 * SWEEPS) % (SUBLANES // 2) == 0
    )


def solution(mesh):
    n_row, n_col = mesh.shape["row"], mesh.shape["col"]

    def local(source, coefficient):
        if fits_kernel(n_row, n_col, source):
            return local_kernel(n_row, n_col, source, coefficient)
        return local_general(source, coefficient)

    return jax.shard_map(
        local,
        mesh=mesh,
        in_specs=(P("row", "col", None), P("row", "col", None)),
        out_specs=P("row", "col", None),
        check_vma=False,
    )
```

```python
import jax
import jax.numpy as jnp
import numpy as np
from jax import lax
from jax.experimental import pallas as pl
from jax.experimental.pallas import tpu as pltpu
from jax.sharding import PartitionSpec as P

SWEEPS = 4


DAMPING = 0.8
SCREEN_SHIFT = 0.02
HIGHEST = lax.Precision.HIGHEST


def padded(block, sides, width):
    for axis, dim in sides:
        count = lax.axis_size(axis)
        forward = [(i, i + 1) for i in range(count - 1)]
        backward = [(target, source) for source, target in forward]
        low = lax.ppermute(
            lax.slice_in_dim(block, block.shape[dim] - width, None, axis=dim), axis, forward
        )
        high = lax.ppermute(lax.slice_in_dim(block, 0, width, axis=dim), axis, backward)
        block = jnp.concatenate([low, block, high], axis=dim)
    return block


def sine_table(length):
    series = jnp.arange(length, dtype=jnp.int32) + 1
    phases = series[:, None] * series[None, :] % (2 * (length + 1))
    return jnp.sin(jnp.pi * phases.astype(jnp.float32) / (length + 1))


def eigenvalues(positions, length):
    angles = jnp.pi * (positions + 1).astype(jnp.float32) / (2 * (length + 1))
    return 4.0 * jnp.sin(angles) ** 2


def neighbour_image(wide_field, diagonal_total):
    zpadded = jnp.pad(wide_field, ((0, 0), (0, 0), (1, 1)))
    center = wide_field[1:-1, 1:-1, :]
    beside = (
        wide_field[2:, 1:-1] + wide_field[:-2, 1:-1] + wide_field[1:-1, 2:] + wide_field[1:-1, :-2]
    )
    beside = beside + zpadded[1:-1, 1:-1, 2:] + zpadded[1:-1, 1:-1, :-2]
    return (center, diagonal_total * center - beside)


def relax_once(wide_field, diagonal_total, source):
    center, applied = neighbour_image(wide_field, diagonal_total)
    return center + DAMPING * (source - applied) / diagonal_total


def trim_rim(tensor, margin):
    return tensor[margin : tensor.shape[0] - margin, margin : tensor.shape[1] - margin]


def inside_table(row_cells, col_cells, margin):
    row_ids = (
        lax.axis_index("row") * row_cells
        - margin
        + jnp.arange(row_cells + 2 * margin, dtype=jnp.int32)
    )
    col_ids = (
        lax.axis_index("col") * col_cells
        - margin
        + jnp.arange(col_cells + 2 * margin, dtype=jnp.int32)
    )
    row_inside = (row_ids >= 0) & (row_ids < row_cells * lax.axis_size("row"))
    col_inside = (col_ids >= 0) & (col_ids < col_cells * lax.axis_size("col"))
    return (row_inside[:, None] & col_inside[None, :]).astype(jnp.float32)[:, :, None]


def coarse_solve(residual):
    row_cells, col_cells, z_cells = residual.shape
    coarse_rows = row_cells // 2
    coarse_cols = col_cells // 2
    coarse_z = z_cells // 2
    total_r = coarse_rows * lax.axis_size("row")
    total_c = coarse_cols * lax.axis_size("col")
    z_slab = coarse_z // lax.axis_size("row")
    r_slab = total_r // lax.axis_size("col")
    coarse = residual.reshape(coarse_rows, 2, coarse_cols, 2, coarse_z, 2).sum(axis=(1, 3, 5)) * 0.5
    table_z = sine_table(coarse_z)
    table_r = sine_table(total_r)
    table_c = sine_table(total_c)
    ordered = jnp.transpose(coarse, (2, 1, 0))
    along_z = jnp.dot(table_z, ordered.reshape(coarse_z, -1), precision=HIGHEST).reshape(
        coarse_z, coarse_cols, coarse_rows
    )
    row_lines = lax.all_to_all(along_z, "row", split_axis=0, concat_axis=2, tiled=True)
    along_r = jnp.einsum("zcr,kr->zkc", row_lines, table_r, precision=HIGHEST)
    col_lines = lax.all_to_all(along_r, "col", split_axis=1, concat_axis=2, tiled=True)
    spectrum = jnp.dot(col_lines.reshape(-1, total_c), table_c, precision=HIGHEST).reshape(
        z_slab, r_slab, total_c
    )
    normaliser = (coarse_z + 1.0) * (total_r + 1.0) * (total_c + 1.0) / 8.0
    lam_z = eigenvalues(
        lax.axis_index("row") * z_slab + jnp.arange(z_slab, dtype=jnp.int32), coarse_z
    )
    lam_r = eigenvalues(
        lax.axis_index("col") * r_slab + jnp.arange(r_slab, dtype=jnp.int32), total_r
    )
    lam_c = eigenvalues(jnp.arange(total_c, dtype=jnp.int32), total_c)
    denominator = (
        SCREEN_SHIFT + lam_z[:, None, None] + lam_r[None, :, None] + lam_c[None, None, :]
    ) * normaliser
    scaled = spectrum / denominator
    back_c = jnp.dot(scaled.reshape(-1, total_c), table_c, precision=HIGHEST).reshape(
        z_slab, r_slab, total_c
    )
    returned = lax.all_to_all(back_c, "col", split_axis=2, concat_axis=1, tiled=True)
    back_r = jnp.einsum("zkc,kr->zcr", returned, table_r, precision=HIGHEST)
    owned = lax.all_to_all(back_r, "row", split_axis=2, concat_axis=0, tiled=True)
    back_z = jnp.dot(table_z, owned.reshape(coarse_z, -1), precision=HIGHEST).reshape(
        coarse_z, coarse_cols, coarse_rows
    )
    correction = jnp.transpose(back_z, (2, 1, 0))
    return jnp.broadcast_to(
        correction[:, None, :, None, :, None], (coarse_rows, 2, coarse_cols, 2, coarse_z, 2)
    ).reshape(row_cells, col_cells, z_cells)


def local_general(source, coefficient):
    row_cells, col_cells, z_cells = source.shape
    diagonal_total = 6.0 + coefficient
    opening = DAMPING * source / diagonal_total
    wide_first, wide_source, wide_coef = (
        padded(opening, (("row", 0), ("col", 1)), SWEEPS),
        padded(source, (("row", 0), ("col", 1)), SWEEPS),
        padded(coefficient, (("row", 0), ("col", 1)), SWEEPS),
    )
    wide_diag = 6.0 + wide_coef
    inside = inside_table(row_cells, col_cells, SWEEPS)
    wide_iter = wide_first
    for repeat in range(1, SWEEPS):
        wide_iter = relax_once(
            wide_iter, trim_rim(wide_diag, repeat), trim_rim(wide_source, repeat)
        ) * trim_rim(inside, repeat)
    iterate, applied = neighbour_image(wide_iter, diagonal_total)
    residual = source - applied
    iterate = iterate + coarse_solve(residual)
    wide_iter = padded(iterate, (("row", 0), ("col", 1)), SWEEPS)
    for repeat in range(1, SWEEPS + 1):
        wide_iter = relax_once(
            wide_iter, trim_rim(wide_diag, repeat), trim_rim(wide_source, repeat)
        ) * trim_rim(inside, repeat)
    return wide_iter


MESH = pl.DeviceIdType.MESH
SUBLANES = 8
MOST_ROWS = 40


def plain_sine(length):
    series = np.arange(length) + 1
    phases = series[:, None] * series[None, :] % (2 * (length + 1))
    return np.sin(np.pi * phases / (length + 1))


def plain_eigen(length):
    return 4.0 * np.sin(np.pi * (np.arange(length) + 1) / (2 * (length + 1))) ** 2


def solve_tables(n_row, n_col, kept, coarse_rows, coarse_cols, coarse_z):
    blocks = n_col * kept
    total_r, total_c = n_row * coarse_rows, n_col * coarse_cols
    sine_z, sine_r, sine_c = plain_sine(coarse_z), plain_sine(total_r), plain_sine(total_c)
    table_z = np.repeat(sine_z, 2, axis=1)
    forward_r = np.zeros((total_r, n_row, blocks))
    forward_r[:, :, :coarse_rows] = sine_r.reshape(total_r, n_row, coarse_rows)
    window_r = np.zeros((n_row, blocks, total_r))
    margin = (blocks - coarse_rows) // 2
    for r in range(n_row):
        for a in range(blocks):
            at = coarse_rows * r - margin + a
            if 0 <= at < total_r:
                window_r[r, a] = sine_r[at]
    table_c = np.zeros((n_col, kept, coarse_cols, kept, total_c))
    for k in range(kept):
        table_c[:, k, :, k, :] = sine_c.reshape(n_col, coarse_cols, total_c)
    normaliser = (coarse_z + 1.0) * (total_r + 1.0) * (total_c + 1.0) / 8.0
    base = SCREEN_SHIFT + plain_eigen(total_r)[:, None] + np.tile(plain_eigen(total_c), kept)[None, :]
    lam_z = np.repeat(plain_eigen(coarse_z).reshape(n_row * n_col, 1, kept), total_c, axis=2)
    lanes = kept * total_c
    tables = (
        table_z,
        forward_r.reshape(total_r, n_row * blocks),
        window_r.reshape(n_row * blocks, total_r),
        table_c.reshape(lanes, lanes),
        base * 2.0 * normaliser,
        lam_z * 2.0 * normaliser,
    )
    return tuple(np.asarray(t, np.float32) for t in tables)


def block_transpose(x, width):
    rows, lanes = x.shape
    row = lax.broadcasted_iota(jnp.int32, x.shape, 0)
    group = lax.broadcasted_iota(jnp.int32, x.shape, 1) // width
    step = 1
    while step < rows:
        row_bit = (row & step) != 0
        group_bit = (group & step) != 0
        from_below = pltpu.roll(pltpu.roll(x, width * step, 1), rows - step, 0)
        from_above = pltpu.roll(pltpu.roll(x, lanes - width * step, 1), step, 0)
        x = jnp.where(row_bit == group_bit, x, jnp.where(group_bit, from_below, from_above))
        step *= 2
    return x


def exact_dot(a, b, contract):
    return lax.dot_general(
        a, b, (contract, ((), ())), precision=HIGHEST, preferred_element_type=jnp.float32
    )


def step_kernel(
    sizes,
    source,
    coefficient,
    table_z_in,
    forward_r_in,
    window_r_in,
    table_c_in,
    base_in,
    lam_z_in,
    out,
    table_z,
    forward_r,
    window_r,
    table_c,
    base,
    lam_z,
    wide_s,
    wide_c,
    weight,
    first,
    field_a,
    field_b,
    rows_sum,
    fine_corr,
    edge,
    send_a,
    recv_a,
    send_b,
    recv_b,
    own_sem,
    table_sem,
    halo_send,
    halo_recv,
    edge_send,
    edge_recv,
    fwd_send,
    fwd_recv,
    back_send,
    back_recv,
    ready,
):
    n_row, n_col, kept = sizes
    row_cells, col_cells, z_cells = source.shape
    coarse_rows, coarse_cols = row_cells // 2, col_cells // 2
    blocks = n_col * kept
    devices = n_row * n_col
    halo_r, halo_c = (wide_s.shape[0] - row_cells) // 2, SUBLANES
    wide_cols = wide_s.shape[1]
    my_row, my_col = lax.axis_index("row"), lax.axis_index("col")
    me = my_row * n_col + my_col

    steps = [(dr, dc) for dr in (-1, 0, 1) for dc in (-1, 0, 1) if (dr, dc) != (0, 0)]

    def exists(dr, dc):
        r, c = my_row + dr, my_col + dc
        return (r >= 0) & (r < n_row) & (c >= 0) & (c < n_col)

    barrier = pltpu.get_barrier_semaphore()
    for d in range(1, n_row):
        pl.semaphore_signal(
            barrier, 1, device_id=(lax.rem(my_row + d, n_row), my_col), device_id_type=MESH
        )
    for d in range(1, n_col):
        pl.semaphore_signal(
            barrier, 1, device_id=(my_row, lax.rem(my_col + d, n_col)), device_id_type=MESH
        )
    greeted = n_row + n_col - 2
    for dr, dc in steps:
        if dr and dc:
            there = exists(dr, dc)

            @pl.when(there)
            def _():
                pl.semaphore_signal(
                    barrier, 1, device_id=(my_row + dr, my_col + dc), device_id_type=MESH
                )

            greeted = greeted + there.astype(jnp.int32)

    arrays = ((source, wide_s), (coefficient, wide_c))
    own = [
        pltpu.make_async_copy(
            here, wide.at[pl.ds(halo_r, row_cells), pl.ds(0, col_cells)], own_sem.at[n]
        )
        for n, (here, wide) in enumerate(arrays)
    ]
    for copy in own:
        copy.start()
    staged = [
        pltpu.make_async_copy(given, held, table_sem.at[n])
        for n, (given, held) in enumerate(
            (
                (table_z_in, table_z),
                (forward_r_in, forward_r),
                (window_r_in, window_r),
                (table_c_in, table_c),
                (base_in, base),
                (lam_z_in, lam_z),
            )
        )
    ]
    for copy in staged:
        copy.start()

    def landing(dr, dc):
        rows = {-1: (0, halo_r), 0: (halo_r, row_cells), 1: (halo_r + row_cells, halo_r)}[dr]
        cols = {
            -1: (col_cells + halo_c, halo_c),
            0: (0, col_cells),
            1: (col_cells, halo_c),
        }[dc]
        return pl.ds(*rows), pl.ds(*cols)

    def leaving(dr, dc):
        rows = {-1: (0, halo_r), 0: (0, row_cells), 1: (row_cells - halo_r, halo_r)}[dr]
        cols = {-1: (0, halo_c), 0: (0, col_cells), 1: (col_cells - halo_c, halo_c)}[dc]
        return pl.ds(*rows), pl.ds(*cols)

    def halo_copies(dr, dc):
        at = steps.index((dr, dc))
        return [
            pltpu.make_async_remote_copy(
                src_ref=here.at[leaving(dr, dc)],
                dst_ref=wide.at[landing(-dr, -dc)],
                send_sem=halo_send.at[n, at],
                recv_sem=halo_recv.at[n, at],
                device_id=(my_row + dr, my_col + dc),
                device_id_type=MESH,
            )
            for n, (here, wide) in enumerate(arrays)
        ]

    pl.semaphore_wait(barrier, greeted)
    for step in steps:

        @pl.when(exists(*step))
        def _():
            for copy in halo_copies(*step):
                copy.start()

    for d in range(1, n_row):
        pl.semaphore_signal(
            ready, 1, device_id=(lax.rem(my_row + d, n_row), my_col), device_id_type=MESH
        )
    for step in steps:

        @pl.when(jnp.logical_not(exists(*step)))
        def _():
            rows, cols = landing(*step)
            for _, wide in arrays:
                wide[rows, cols] = jnp.zeros((rows.size, cols.size, z_cells), jnp.float32)

    for copy in own:
        copy.wait()
    for dr, dc in steps:
        @pl.when(exists(-dr, -dc))
        def _():
            for copy in halo_copies(dr, dc):
                copy.wait_recv()

    wide_rows = wide_s.shape[0]
    col_at = lax.broadcasted_iota(jnp.int32, (wide_cols, z_cells), 0)
    z_at = lax.broadcasted_iota(jnp.int32, (wide_cols, z_cells), 1)
    col_at = my_col * col_cells + jnp.where(col_at >= col_cells + halo_c, col_at - wide_cols, col_at)
    col_inside = (col_at >= 0) & (col_at < n_col * col_cells)
    not_first = z_at > 0
    not_last = z_at < z_cells - 1

    def prepare(i):
        at = my_row * row_cells + i - halo_r
        inside = (at >= 0) & (at < n_row * row_cells)
        scale = jnp.where(inside & col_inside, DAMPING / (6.0 + wide_c[i]), 0.0)
        weight[i] = scale
        first[i] = scale * wide_s[i]

    piece = SUBLANES // 2

    @pl.loop(0, wide_rows // piece)
    def _(n):
        for m in range(piece):
            prepare(n * piece + m)

    def beside(above, here, below):
        cols = here.shape[0]
        low = jnp.where(not_first[:cols], pltpu.roll(here, 1, 1), 0.0)
        high = jnp.where(not_last[:cols], pltpu.roll(here, z_cells - 1, 1), 0.0)
        return (
            (above + below)
            + (pltpu.roll(here, 1, 0) + pltpu.roll(here, cols - 1, 0))
            + (low + high)
        )

    def sweep(old, new, low, high, shift=0, cols=wide_cols):
        chunk = max(m for m in range(1, MOST_ROWS + 1) if (high - low) % m == 0)

        def work(i):
            lines = [old[i - 1 + m] for m in range(chunk + 2)]
            for m in range(chunk):
                here = lines[m + 1]
                fresh = (1.0 - DAMPING) * here + (
                    first[i + m] + weight[i + m] * beside(lines[m], here, lines[m + 2])
                )
                new[i + m - shift] = fresh[:cols]

        if chunk == high - low:
            work(low)
        else:

            @pl.loop(0, (high - low) // chunk)
            def _(n):
                work(low + n * chunk)

    fields = (first,) + (field_b, field_a) * SWEEPS
    smooth, other = fields[SWEEPS - 1], fields[SWEEPS]
    for turn in range(1, SWEEPS):
        sweep(fields[turn - 1], fields[turn], turn, wide_rows - turn)

    edge_rows = halo_r - 1
    edge_at = (0, halo_r + row_cells + 1)

    def edge_copy(dr):
        return pltpu.make_async_remote_copy(
            src_ref=smooth.at[
                pl.ds(halo_r + (1 if dr < 0 else row_cells - halo_r), edge_rows)
            ],
            dst_ref=edge.at[1 if dr < 0 else 0],
            send_sem=edge_send.at[1 if dr < 0 else 0],
            recv_sem=edge_recv.at[1 if dr < 0 else 0],
            device_id=(my_row + dr, my_col),
            device_id_type=MESH,
        )

    def start_edges():
        for dr in (-1, 1):

            @pl.when(exists(dr, 0))
            def _():
                edge_copy(dr).start()

    @pl.loop(0, coarse_rows)
    def _(a):
        i = halo_r + 2 * a
        lines = [smooth[i - 1 + m] for m in range(4)]
        total = None
        for m in range(2):
            near = beside(lines[m], lines[m + 1], lines[m + 2])
            left = wide_s[i + m] + (near - (6.0 + wide_c[i + m]) * lines[m + 1])
            total = left if total is None else total + left
        rows_sum[a] = total[:col_cells]

    for copy in staged:
        copy.wait()
    pairs = [
        rows_sum[a, pl.ds(0, coarse_cols, stride=2), :]
        + rows_sum[a, pl.ds(1, coarse_cols, stride=2), :]
        for a in range(coarse_rows)
    ]
    blank = jnp.zeros(((blocks - coarse_rows) * coarse_cols, z_cells), jnp.float32)
    along_z = exact_dot(
        table_z[...], jnp.concatenate(pairs + [blank], axis=0), ((1,), (1,))
    )
    for q in range(devices):
        send_a[q] = along_z[q * kept : (q + 1) * kept]

    pl.semaphore_wait(ready, n_row - 1)

    def exchange(send, recv, send_sem, recv_sem, meanwhile=None):
        def copy(d):
            target = lax.rem(me + d, devices)
            return pltpu.make_async_remote_copy(
                src_ref=send.at[target],
                dst_ref=recv.at[me],
                send_sem=send_sem.at[d],
                recv_sem=recv_sem.at[d],
                device_id=(lax.div(target, n_col), lax.rem(target, n_col)),
                device_id_type=MESH,
            )

        @pl.loop(1, devices)
        def _(d):
            copy(d).start()

        recv[me] = send[me]
        if meanwhile is not None:
            meanwhile()

        @pl.loop(1, devices)
        def _(d):
            copy(d).wait_recv()

        return copy

    forward = exchange(send_a, recv_a, fwd_send, fwd_recv, start_edges)

    gathered = jnp.concatenate(
        [
            block_transpose(
                recv_a[pl.ds(r * n_col, n_col)].reshape(blocks, z_cells), coarse_cols
            )
            for r in range(n_row)
        ],
        axis=0,
    )
    along_r = exact_dot(forward_r[...], gathered, ((1,), (0,)))
    spectrum = exact_dot(along_r, table_c[...], ((1,), (0,)))
    scaled = spectrum / (base[...] + lam_z[me])
    back_c = exact_dot(scaled, table_c[...], ((1,), (1,)))
    back_r = exact_dot(window_r[...], back_c, ((1,), (0,)))
    lane = lax.broadcasted_iota(jnp.int32, (blocks, z_cells), 1)
    column = lane // (kept * coarse_cols)
    late = lane % coarse_cols >= coarse_cols // 2
    for r in range(n_row):
        plane = back_r[r * blocks : (r + 1) * blocks]
        right = jnp.where(
            column < n_col - 1, pltpu.roll(plane, z_cells - kept * coarse_cols, 1), 0.0
        )
        left = jnp.where(column > 0, pltpu.roll(plane, kept * coarse_cols, 1), 0.0)
        at = pl.ds(r * n_col, n_col)
        send_b[at, pl.ds(0, kept)] = block_transpose(plane, coarse_cols).reshape(
            n_col, kept, z_cells
        )
        send_b[at, pl.ds(kept, kept)] = block_transpose(
            jnp.where(late, left, right), coarse_cols
        ).reshape(n_col, kept, z_cells)

    backward = exchange(send_b, recv_b, back_send, back_recv)

    modes = devices * kept
    for part in range(2):
        lines = recv_b[:, pl.ds(part * kept, kept)].reshape(modes, z_cells)
        values = exact_dot(jnp.transpose(lines), table_z[...], ((1,), (0,)))
        for a in range(blocks):
            for odd in range(2):
                fine_corr[a, pl.ds(part * col_cells + odd, coarse_cols, stride=2), :] = values[
                    a * coarse_cols : (a + 1) * coarse_cols
                ]

    for dr in (-1, 1):
        slot = 1 if dr < 0 else 0

        @pl.when(exists(dr, 0))
        def _():
            edge_copy(dr).wait_send()

        @pl.when(exists(-dr, 0))
        def _():
            edge_copy(dr).wait_recv()
            smooth[pl.ds(edge_at[slot], edge_rows)] = edge[slot]

        @pl.when(jnp.logical_not(exists(-dr, 0)))
        def _():
            smooth[pl.ds(edge_at[slot], edge_rows)] = jnp.zeros(edge.shape[1:], jnp.float32)

    margin = halo_r - (blocks - coarse_rows)

    @pl.loop(0, blocks)
    def _(a):
        i = margin + 2 * a
        smooth[i] = smooth[i] + fine_corr[a]
        smooth[i + 1] = smooth[i + 1] + fine_corr[a]

    fields = (smooth, other) * SWEEPS
    for turn in range(SWEEPS):
        low, high = margin + 1 + turn, wide_rows - margin - 1 - turn
        if turn < SWEEPS - 1:
            sweep(fields[turn], fields[turn + 1], low, high)
        else:
            sweep(fields[turn], out, low, high, low, col_cells)

    for step in steps:

        @pl.when(exists(*step))
        def _():
            for copy in halo_copies(*step):
                copy.wait_send()

    @pl.loop(1, devices)
    def _(d):
        forward(d).wait_send()
        backward(d).wait_send()


def local_kernel(n_row, n_col, source, coefficient):
    row_cells, col_cells, z_cells = source.shape
    coarse_rows, coarse_cols, coarse_z = row_cells // 2, col_cells // 2, z_cells // 2
    devices = n_row * n_col
    kept = coarse_z // devices
    blocks = n_col * kept
    tables = solve_tables(n_row, n_col, kept, coarse_rows, coarse_cols, coarse_z)
    wide = (row_cells + 2 * SWEEPS, col_cells + 2 * SUBLANES, z_cells)
    dma = pltpu.SemaphoreType.DMA
    f32 = jnp.float32

    def body(*refs):
        step_kernel((n_row, n_col, kept), *refs)

    return pl.pallas_call(
        body,
        out_shape=jax.ShapeDtypeStruct(source.shape, f32),
        in_specs=[pl.BlockSpec(memory_space=pl.ANY)] * (2 + len(tables)),
        out_specs=pl.BlockSpec(memory_space=pltpu.VMEM),
        scratch_shapes=[pltpu.VMEM(t.shape, f32) for t in tables]
        + [pltpu.VMEM(wide, f32)] * 6
        + [
            pltpu.VMEM((coarse_rows, col_cells, z_cells), f32),
            pltpu.VMEM((blocks, 2 * col_cells, z_cells), f32),
            pltpu.VMEM((2, SWEEPS - 1) + wide[1:], f32),
            pltpu.VMEM((devices, kept, z_cells), f32),
            pltpu.VMEM((devices, kept, z_cells), f32),
            pltpu.VMEM((devices, 2 * kept, z_cells), f32),
            pltpu.VMEM((devices, 2 * kept, z_cells), f32),
            dma((2,)),
            dma((len(tables),)),
            dma((2, 8)),
            dma((2, 8)),
            dma((2,)),
            dma((2,)),
            dma((devices,)),
            dma((devices,)),
            dma((devices,)),
            dma((devices,)),
            pltpu.SemaphoreType.REGULAR,
        ],
        compiler_params=pltpu.CompilerParams(collective_id=0, has_side_effects=True),
        name="vstep",
    )(source, coefficient, *(jnp.asarray(t) for t in tables))


def fits_kernel(n_row, n_col, source):
    row_cells, col_cells, z_cells = source.shape
    devices = n_row * n_col
    kept = (z_cells // 2) // devices
    blocks = n_col * kept
    return (
        kept * devices * 2 == z_cells
        and z_cells == 128
        and col_cells == 2 * SUBLANES
        and blocks * (col_cells // 2) == z_cells
        and blocks == row_cells // 2 + SWEEPS
        and row_cells >= 2 * SWEEPS
        and (row_cells + 2 * SWEEPS) % (SUBLANES // 2) == 0
    )


def solution(mesh):
    n_row, n_col = mesh.shape["row"], mesh.shape["col"]

    def local(source, coefficient):
        if fits_kernel(n_row, n_col, source):
            return local_kernel(n_row, n_col, source, coefficient)
        return local_general(source, coefficient)

    return jax.shard_map(
        local,
        mesh=mesh,
        in_specs=(P("row", "col", None), P("row", "col", None)),
        out_specs=P("row", "col", None),
        check_vma=False,
    )
```

```python
import jax
import jax.numpy as jnp
import numpy as np
from jax import lax
from jax.experimental import pallas as pl
from jax.experimental.pallas import tpu as pltpu
from jax.sharding import PartitionSpec as P

SWEEPS = 4


DAMPING = 0.8
SCREEN_SHIFT = 0.02
HIGHEST = lax.Precision.HIGHEST


def padded(block, sides, width):
    for axis, dim in sides:
        count = lax.axis_size(axis)
        forward = [(i, i + 1) for i in range(count - 1)]
        backward = [(target, source) for source, target in forward]
        low = lax.ppermute(
            lax.slice_in_dim(block, block.shape[dim] - width, None, axis=dim), axis, forward
        )
        high = lax.ppermute(lax.slice_in_dim(block, 0, width, axis=dim), axis, backward)
        block = jnp.concatenate([low, block, high], axis=dim)
    return block


def sine_table(length):
    series = jnp.arange(length, dtype=jnp.int32) + 1
    phases = series[:, None] * series[None, :] % (2 * (length + 1))
    return jnp.sin(jnp.pi * phases.astype(jnp.float32) / (length + 1))


def eigenvalues(positions, length):
    angles = jnp.pi * (positions + 1).astype(jnp.float32) / (2 * (length + 1))
    return 4.0 * jnp.sin(angles) ** 2


def neighbour_image(wide_field, diagonal_total):
    zpadded = jnp.pad(wide_field, ((0, 0), (0, 0), (1, 1)))
    center = wide_field[1:-1, 1:-1, :]
    beside = (
        wide_field[2:, 1:-1] + wide_field[:-2, 1:-1] + wide_field[1:-1, 2:] + wide_field[1:-1, :-2]
    )
    beside = beside + zpadded[1:-1, 1:-1, 2:] + zpadded[1:-1, 1:-1, :-2]
    return (center, diagonal_total * center - beside)


def relax_once(wide_field, diagonal_total, source):
    center, applied = neighbour_image(wide_field, diagonal_total)
    return center + DAMPING * (source - applied) / diagonal_total


def trim_rim(tensor, margin):
    return tensor[margin : tensor.shape[0] - margin, margin : tensor.shape[1] - margin]


def inside_table(row_cells, col_cells, margin):
    row_ids = (
        lax.axis_index("row") * row_cells
        - margin
        + jnp.arange(row_cells + 2 * margin, dtype=jnp.int32)
    )
    col_ids = (
        lax.axis_index("col") * col_cells
        - margin
        + jnp.arange(col_cells + 2 * margin, dtype=jnp.int32)
    )
    row_inside = (row_ids >= 0) & (row_ids < row_cells * lax.axis_size("row"))
    col_inside = (col_ids >= 0) & (col_ids < col_cells * lax.axis_size("col"))
    return (row_inside[:, None] & col_inside[None, :]).astype(jnp.float32)[:, :, None]


def coarse_solve(residual):
    row_cells, col_cells, z_cells = residual.shape
    coarse_rows = row_cells // 2
    coarse_cols = col_cells // 2
    coarse_z = z_cells // 2
    total_r = coarse_rows * lax.axis_size("row")
    total_c = coarse_cols * lax.axis_size("col")
    z_slab = coarse_z // lax.axis_size("row")
    r_slab = total_r // lax.axis_size("col")
    coarse = residual.reshape(coarse_rows, 2, coarse_cols, 2, coarse_z, 2).sum(axis=(1, 3, 5)) * 0.5
    table_z = sine_table(coarse_z)
    table_r = sine_table(total_r)
    table_c = sine_table(total_c)
    ordered = jnp.transpose(coarse, (2, 1, 0))
    along_z = jnp.dot(table_z, ordered.reshape(coarse_z, -1), precision=HIGHEST).reshape(
        coarse_z, coarse_cols, coarse_rows
    )
    row_lines = lax.all_to_all(along_z, "row", split_axis=0, concat_axis=2, tiled=True)
    along_r = jnp.einsum("zcr,kr->zkc", row_lines, table_r, precision=HIGHEST)
    col_lines = lax.all_to_all(along_r, "col", split_axis=1, concat_axis=2, tiled=True)
    spectrum = jnp.dot(col_lines.reshape(-1, total_c), table_c, precision=HIGHEST).reshape(
        z_slab, r_slab, total_c
    )
    normaliser = (coarse_z + 1.0) * (total_r + 1.0) * (total_c + 1.0) / 8.0
    lam_z = eigenvalues(
        lax.axis_index("row") * z_slab + jnp.arange(z_slab, dtype=jnp.int32), coarse_z
    )
    lam_r = eigenvalues(
        lax.axis_index("col") * r_slab + jnp.arange(r_slab, dtype=jnp.int32), total_r
    )
    lam_c = eigenvalues(jnp.arange(total_c, dtype=jnp.int32), total_c)
    denominator = (
        SCREEN_SHIFT + lam_z[:, None, None] + lam_r[None, :, None] + lam_c[None, None, :]
    ) * normaliser
    scaled = spectrum / denominator
    back_c = jnp.dot(scaled.reshape(-1, total_c), table_c, precision=HIGHEST).reshape(
        z_slab, r_slab, total_c
    )
    returned = lax.all_to_all(back_c, "col", split_axis=2, concat_axis=1, tiled=True)
    back_r = jnp.einsum("zkc,kr->zcr", returned, table_r, precision=HIGHEST)
    owned = lax.all_to_all(back_r, "row", split_axis=2, concat_axis=0, tiled=True)
    back_z = jnp.dot(table_z, owned.reshape(coarse_z, -1), precision=HIGHEST).reshape(
        coarse_z, coarse_cols, coarse_rows
    )
    correction = jnp.transpose(back_z, (2, 1, 0))
    return jnp.broadcast_to(
        correction[:, None, :, None, :, None], (coarse_rows, 2, coarse_cols, 2, coarse_z, 2)
    ).reshape(row_cells, col_cells, z_cells)


def local_general(source, coefficient):
    row_cells, col_cells, z_cells = source.shape
    diagonal_total = 6.0 + coefficient
    opening = DAMPING * source / diagonal_total
    wide_first, wide_source, wide_coef = (
        padded(opening, (("row", 0), ("col", 1)), SWEEPS),
        padded(source, (("row", 0), ("col", 1)), SWEEPS),
        padded(coefficient, (("row", 0), ("col", 1)), SWEEPS),
    )
    wide_diag = 6.0 + wide_coef
    inside = inside_table(row_cells, col_cells, SWEEPS)
    wide_iter = wide_first
    for repeat in range(1, SWEEPS):
        wide_iter = relax_once(
            wide_iter, trim_rim(wide_diag, repeat), trim_rim(wide_source, repeat)
        ) * trim_rim(inside, repeat)
    iterate, applied = neighbour_image(wide_iter, diagonal_total)
    residual = source - applied
    iterate = iterate + coarse_solve(residual)
    wide_iter = padded(iterate, (("row", 0), ("col", 1)), SWEEPS)
    for repeat in range(1, SWEEPS + 1):
        wide_iter = relax_once(
            wide_iter, trim_rim(wide_diag, repeat), trim_rim(wide_source, repeat)
        ) * trim_rim(inside, repeat)
    return wide_iter


MESH = pl.DeviceIdType.MESH
SUBLANES = 8
MOST_ROWS = 40


def plain_sine(length):
    series = np.arange(length) + 1
    phases = series[:, None] * series[None, :] % (2 * (length + 1))
    return np.sin(np.pi * phases / (length + 1))


def plain_eigen(length):
    return 4.0 * np.sin(np.pi * (np.arange(length) + 1) / (2 * (length + 1))) ** 2


def solve_tables(n_row, n_col, kept, coarse_rows, coarse_cols, coarse_z):
    blocks = n_col * kept
    total_r, total_c = n_row * coarse_rows, n_col * coarse_cols
    sine_z, sine_r, sine_c = plain_sine(coarse_z), plain_sine(total_r), plain_sine(total_c)
    table_z = np.repeat(sine_z, 2, axis=1)
    forward_r = np.zeros((total_r, n_row, blocks))
    forward_r[:, :, :coarse_rows] = sine_r.reshape(total_r, n_row, coarse_rows)
    window_r = np.zeros((n_row, blocks, total_r))
    margin = (blocks - coarse_rows) // 2
    for r in range(n_row):
        for a in range(blocks):
            at = coarse_rows * r - margin + a
            if 0 <= at < total_r:
                window_r[r, a] = sine_r[at]
    table_c = np.zeros((n_col, kept, coarse_cols, kept, total_c))
    for k in range(kept):
        table_c[:, k, :, k, :] = sine_c.reshape(n_col, coarse_cols, total_c)
    normaliser = (coarse_z + 1.0) * (total_r + 1.0) * (total_c + 1.0) / 8.0
    base = SCREEN_SHIFT + plain_eigen(total_r)[:, None] + np.tile(plain_eigen(total_c), kept)[None, :]
    lam_z = np.repeat(plain_eigen(coarse_z).reshape(n_row * n_col, 1, kept), total_c, axis=2)
    lanes = kept * total_c
    tables = (
        table_z,
        forward_r.reshape(total_r, n_row * blocks),
        window_r.reshape(n_row * blocks, total_r),
        table_c.reshape(lanes, lanes),
        base * 2.0 * normaliser,
        lam_z * 2.0 * normaliser,
    )
    return tuple(np.asarray(t, np.float32) for t in tables)


def block_transpose(x, width):
    rows, lanes = x.shape
    row = lax.broadcasted_iota(jnp.int32, x.shape, 0)
    group = lax.broadcasted_iota(jnp.int32, x.shape, 1) // width
    step = 1
    while step < rows:
        row_bit = (row & step) != 0
        group_bit = (group & step) != 0
        from_below = pltpu.roll(pltpu.roll(x, width * step, 1), rows - step, 0)
        from_above = pltpu.roll(pltpu.roll(x, lanes - width * step, 1), step, 0)
        x = jnp.where(row_bit == group_bit, x, jnp.where(group_bit, from_below, from_above))
        step *= 2
    return x


def split_dot(a, b, contract):
    def parts(x):
        high = x.astype(jnp.bfloat16)
        return high, (x - high.astype(jnp.float32)).astype(jnp.bfloat16)

    def product(x, y):
        return lax.dot_general(x, y, (contract, ((), ())), preferred_element_type=jnp.float32)

    (a_high, a_low), (b_high, b_low) = parts(a), parts(b)
    return product(a_high, b_high) + (product(a_high, b_low) + product(a_low, b_high))


def step_kernel(
    sizes,
    source,
    coefficient,
    table_z_in,
    forward_r_in,
    window_r_in,
    table_c_in,
    base_in,
    lam_z_in,
    out,
    table_z,
    forward_r,
    window_r,
    table_c,
    base,
    lam_z,
    wide_s,
    wide_c,
    weight,
    first,
    field_a,
    field_b,
    rows_sum,
    fine_corr,
    edge,
    send_a,
    recv_a,
    send_b,
    recv_b,
    own_sem,
    table_sem,
    halo_send,
    halo_recv,
    edge_send,
    edge_recv,
    fwd_send,
    fwd_recv,
    back_send,
    back_recv,
    ready,
):
    n_row, n_col, kept = sizes
    row_cells, col_cells, z_cells = source.shape
    coarse_rows, coarse_cols = row_cells // 2, col_cells // 2
    blocks = n_col * kept
    devices = n_row * n_col
    halo_r, halo_c = (wide_s.shape[0] - row_cells) // 2, SUBLANES
    wide_cols = wide_s.shape[1]
    my_row, my_col = lax.axis_index("row"), lax.axis_index("col")
    me = my_row * n_col + my_col

    steps = [(dr, dc) for dr in (-1, 0, 1) for dc in (-1, 0, 1) if (dr, dc) != (0, 0)]

    def exists(dr, dc):
        r, c = my_row + dr, my_col + dc
        return (r >= 0) & (r < n_row) & (c >= 0) & (c < n_col)

    barrier = pltpu.get_barrier_semaphore()
    for d in range(1, n_row):
        pl.semaphore_signal(
            barrier, 1, device_id=(lax.rem(my_row + d, n_row), my_col), device_id_type=MESH
        )
    for d in range(1, n_col):
        pl.semaphore_signal(
            barrier, 1, device_id=(my_row, lax.rem(my_col + d, n_col)), device_id_type=MESH
        )
    greeted = n_row + n_col - 2
    for dr, dc in steps:
        if dr and dc:
            there = exists(dr, dc)

            @pl.when(there)
            def _():
                pl.semaphore_signal(
                    barrier, 1, device_id=(my_row + dr, my_col + dc), device_id_type=MESH
                )

            greeted = greeted + there.astype(jnp.int32)

    arrays = ((source, wide_s), (coefficient, wide_c))
    own = [
        pltpu.make_async_copy(
            here, wide.at[pl.ds(halo_r, row_cells), pl.ds(0, col_cells)], own_sem.at[n]
        )
        for n, (here, wide) in enumerate(arrays)
    ]
    for copy in own:
        copy.start()
    staged = [
        pltpu.make_async_copy(given, held, table_sem.at[n])
        for n, (given, held) in enumerate(
            (
                (table_z_in, table_z),
                (forward_r_in, forward_r),
                (window_r_in, window_r),
                (table_c_in, table_c),
                (base_in, base),
                (lam_z_in, lam_z),
            )
        )
    ]
    for copy in staged:
        copy.start()

    def landing(dr, dc):
        rows = {-1: (0, halo_r), 0: (halo_r, row_cells), 1: (halo_r + row_cells, halo_r)}[dr]
        cols = {
            -1: (col_cells + halo_c, halo_c),
            0: (0, col_cells),
            1: (col_cells, halo_c),
        }[dc]
        return pl.ds(*rows), pl.ds(*cols)

    def leaving(dr, dc):
        rows = {-1: (0, halo_r), 0: (0, row_cells), 1: (row_cells - halo_r, halo_r)}[dr]
        cols = {-1: (0, halo_c), 0: (0, col_cells), 1: (col_cells - halo_c, halo_c)}[dc]
        return pl.ds(*rows), pl.ds(*cols)

    def halo_copies(dr, dc):
        at = steps.index((dr, dc))
        return [
            pltpu.make_async_remote_copy(
                src_ref=here.at[leaving(dr, dc)],
                dst_ref=wide.at[landing(-dr, -dc)],
                send_sem=halo_send.at[n, at],
                recv_sem=halo_recv.at[n, at],
                device_id=(my_row + dr, my_col + dc),
                device_id_type=MESH,
            )
            for n, (here, wide) in enumerate(arrays)
        ]

    pl.semaphore_wait(barrier, greeted)
    for step in steps:

        @pl.when(exists(*step))
        def _():
            for copy in halo_copies(*step):
                copy.start()

    for d in range(1, n_row):
        pl.semaphore_signal(
            ready, 1, device_id=(lax.rem(my_row + d, n_row), my_col), device_id_type=MESH
        )
    for step in steps:

        @pl.when(jnp.logical_not(exists(*step)))
        def _():
            rows, cols = landing(*step)
            for _, wide in arrays:
                wide[rows, cols] = jnp.zeros((rows.size, cols.size, z_cells), jnp.float32)

    for copy in own:
        copy.wait()
    for dr, dc in steps:
        @pl.when(exists(-dr, -dc))
        def _():
            for copy in halo_copies(dr, dc):
                copy.wait_recv()

    wide_rows = wide_s.shape[0]
    col_at = lax.broadcasted_iota(jnp.int32, (wide_cols, z_cells), 0)
    z_at = lax.broadcasted_iota(jnp.int32, (wide_cols, z_cells), 1)
    col_at = my_col * col_cells + jnp.where(col_at >= col_cells + halo_c, col_at - wide_cols, col_at)
    col_inside = (col_at >= 0) & (col_at < n_col * col_cells)
    not_first = z_at > 0
    not_last = z_at < z_cells - 1

    def prepare(i):
        at = my_row * row_cells + i - halo_r
        inside = (at >= 0) & (at < n_row * row_cells)
        scale = jnp.where(inside & col_inside, DAMPING / (6.0 + wide_c[i]), 0.0)
        weight[i] = scale
        first[i] = scale * wide_s[i]

    piece = SUBLANES // 2

    @pl.loop(0, wide_rows // piece)
    def _(n):
        for m in range(piece):
            prepare(n * piece + m)

    def beside(above, here, below):
        cols = here.shape[0]
        low = jnp.where(not_first[:cols], pltpu.roll(here, 1, 1), 0.0)
        high = jnp.where(not_last[:cols], pltpu.roll(here, z_cells - 1, 1), 0.0)
        return (
            (above + below)
            + (pltpu.roll(here, 1, 0) + pltpu.roll(here, cols - 1, 0))
            + (low + high)
        )

    def sweep(old, new, low, high, shift=0, cols=wide_cols):
        chunk = max(m for m in range(1, MOST_ROWS + 1) if (high - low) % m == 0)

        def work(i):
            lines = [old[i - 1 + m] for m in range(chunk + 2)]
            for m in range(chunk):
                here = lines[m + 1]
                fresh = (1.0 - DAMPING) * here + (
                    first[i + m] + weight[i + m] * beside(lines[m], here, lines[m + 2])
                )
                new[i + m - shift] = fresh[:cols]

        if chunk == high - low:
            work(low)
        else:

            @pl.loop(0, (high - low) // chunk)
            def _(n):
                work(low + n * chunk)

    fields = (first,) + (field_b, field_a) * SWEEPS
    smooth, other = fields[SWEEPS - 1], fields[SWEEPS]
    for turn in range(1, SWEEPS):
        sweep(fields[turn - 1], fields[turn], turn, wide_rows - turn)

    edge_rows = halo_r - 1
    edge_at = (0, halo_r + row_cells + 1)

    def edge_copy(dr):
        return pltpu.make_async_remote_copy(
            src_ref=smooth.at[
                pl.ds(halo_r + (1 if dr < 0 else row_cells - halo_r), edge_rows)
            ],
            dst_ref=edge.at[1 if dr < 0 else 0],
            send_sem=edge_send.at[1 if dr < 0 else 0],
            recv_sem=edge_recv.at[1 if dr < 0 else 0],
            device_id=(my_row + dr, my_col),
            device_id_type=MESH,
        )

    def start_edges():
        for dr in (-1, 1):

            @pl.when(exists(dr, 0))
            def _():
                edge_copy(dr).start()

    @pl.loop(0, coarse_rows)
    def _(a):
        i = halo_r + 2 * a
        lines = [smooth[i - 1 + m] for m in range(4)]
        total = None
        for m in range(2):
            near = beside(lines[m], lines[m + 1], lines[m + 2])
            left = wide_s[i + m] + (near - (6.0 + wide_c[i + m]) * lines[m + 1])
            total = left if total is None else total + left
        rows_sum[a] = total[:col_cells]

    for copy in staged:
        copy.wait()
    pairs = [
        rows_sum[a, pl.ds(0, coarse_cols, stride=2), :]
        + rows_sum[a, pl.ds(1, coarse_cols, stride=2), :]
        for a in range(coarse_rows)
    ]
    blank = jnp.zeros(((blocks - coarse_rows) * coarse_cols, z_cells), jnp.float32)
    along_z = split_dot(
        table_z[...], jnp.concatenate(pairs + [blank], axis=0), ((1,), (1,))
    )
    for q in range(devices):
        send_a[q] = along_z[q * kept : (q + 1) * kept]

    pl.semaphore_wait(ready, n_row - 1)

    def exchange(send, recv, send_sem, recv_sem, meanwhile=None):
        def copy(d):
            target = lax.rem(me + d, devices)
            return pltpu.make_async_remote_copy(
                src_ref=send.at[target],
                dst_ref=recv.at[me],
                send_sem=send_sem.at[d],
                recv_sem=recv_sem.at[d],
                device_id=(lax.div(target, n_col), lax.rem(target, n_col)),
                device_id_type=MESH,
            )

        @pl.loop(1, devices, unroll=True)
        def _(d):
            copy(d).start()

        recv[me] = send[me]
        if meanwhile is not None:
            meanwhile()

        @pl.loop(1, devices)
        def _(d):
            copy(d).wait_recv()

        return copy

    forward = exchange(send_a, recv_a, fwd_send, fwd_recv, start_edges)

    gathered = jnp.concatenate(
        [
            block_transpose(
                recv_a[pl.ds(r * n_col, n_col)].reshape(blocks, z_cells), coarse_cols
            )
            for r in range(n_row)
        ],
        axis=0,
    )
    along_r = split_dot(forward_r[...], gathered, ((1,), (0,)))
    spectrum = split_dot(along_r, table_c[...], ((1,), (0,)))
    scaled = spectrum / (base[...] + lam_z[me])
    back_c = split_dot(scaled, table_c[...], ((1,), (1,)))
    back_r = split_dot(window_r[...], back_c, ((1,), (0,)))
    lane = lax.broadcasted_iota(jnp.int32, (blocks, z_cells), 1)
    column = lane // (kept * coarse_cols)
    late = lane % coarse_cols >= coarse_cols // 2
    for r in range(n_row):
        plane = back_r[r * blocks : (r + 1) * blocks]
        right = jnp.where(
            column < n_col - 1, pltpu.roll(plane, z_cells - kept * coarse_cols, 1), 0.0
        )
        left = jnp.where(column > 0, pltpu.roll(plane, kept * coarse_cols, 1), 0.0)
        at = pl.ds(r * n_col, n_col)
        send_b[at, pl.ds(0, kept)] = block_transpose(plane, coarse_cols).reshape(
            n_col, kept, z_cells
        )
        send_b[at, pl.ds(kept, kept)] = block_transpose(
            jnp.where(late, left, right), coarse_cols
        ).reshape(n_col, kept, z_cells)

    backward = exchange(send_b, recv_b, back_send, back_recv)

    modes = devices * kept
    for part in range(2):
        lines = recv_b[:, pl.ds(part * kept, kept)].reshape(modes, z_cells)
        values = split_dot(jnp.transpose(lines), table_z[...], ((1,), (0,)))
        for a in range(blocks):
            for odd in range(2):
                fine_corr[a, pl.ds(part * col_cells + odd, coarse_cols, stride=2), :] = values[
                    a * coarse_cols : (a + 1) * coarse_cols
                ]

    for dr in (-1, 1):
        slot = 1 if dr < 0 else 0

        @pl.when(exists(dr, 0))
        def _():
            edge_copy(dr).wait_send()

        @pl.when(exists(-dr, 0))
        def _():
            edge_copy(dr).wait_recv()
            smooth[pl.ds(edge_at[slot], edge_rows)] = edge[slot]

        @pl.when(jnp.logical_not(exists(-dr, 0)))
        def _():
            smooth[pl.ds(edge_at[slot], edge_rows)] = jnp.zeros(edge.shape[1:], jnp.float32)

    margin = halo_r - (blocks - coarse_rows)

    @pl.loop(0, blocks)
    def _(a):
        i = margin + 2 * a
        smooth[i] = smooth[i] + fine_corr[a]
        smooth[i + 1] = smooth[i + 1] + fine_corr[a]

    fields = (smooth, other) * SWEEPS
    for turn in range(SWEEPS):
        low, high = margin + 1 + turn, wide_rows - margin - 1 - turn
        if turn < SWEEPS - 1:
            sweep(fields[turn], fields[turn + 1], low, high)
        else:
            sweep(fields[turn], out, low, high, low, col_cells)

    for step in steps:

        @pl.when(exists(*step))
        def _():
            for copy in halo_copies(*step):
                copy.wait_send()

    @pl.loop(1, devices)
    def _(d):
        forward(d).wait_send()
        backward(d).wait_send()


def local_kernel(n_row, n_col, source, coefficient):
    row_cells, col_cells, z_cells = source.shape
    coarse_rows, coarse_cols, coarse_z = row_cells // 2, col_cells // 2, z_cells // 2
    devices = n_row * n_col
    kept = coarse_z // devices
    blocks = n_col * kept
    tables = solve_tables(n_row, n_col, kept, coarse_rows, coarse_cols, coarse_z)
    wide = (row_cells + 2 * SWEEPS, col_cells + 2 * SUBLANES, z_cells)
    dma = pltpu.SemaphoreType.DMA
    f32 = jnp.float32

    def body(*refs):
        step_kernel((n_row, n_col, kept), *refs)

    return pl.pallas_call(
        body,
        out_shape=jax.ShapeDtypeStruct(source.shape, f32),
        in_specs=[pl.BlockSpec(memory_space=pl.ANY)] * (2 + len(tables)),
        out_specs=pl.BlockSpec(memory_space=pltpu.VMEM),
        scratch_shapes=[pltpu.VMEM(t.shape, f32) for t in tables]
        + [pltpu.VMEM(wide, f32)] * 6
        + [
            pltpu.VMEM((coarse_rows, col_cells, z_cells), f32),
            pltpu.VMEM((blocks, 2 * col_cells, z_cells), f32),
            pltpu.VMEM((2, SWEEPS - 1) + wide[1:], f32),
            pltpu.VMEM((devices, kept, z_cells), f32),
            pltpu.VMEM((devices, kept, z_cells), f32),
            pltpu.VMEM((devices, 2 * kept, z_cells), f32),
            pltpu.VMEM((devices, 2 * kept, z_cells), f32),
            dma((2,)),
            dma((len(tables),)),
            dma((2, 8)),
            dma((2, 8)),
            dma((2,)),
            dma((2,)),
            dma((devices,)),
            dma((devices,)),
            dma((devices,)),
            dma((devices,)),
            pltpu.SemaphoreType.REGULAR,
        ],
        compiler_params=pltpu.CompilerParams(collective_id=0, has_side_effects=True),
        name="vstep",
    )(source, coefficient, *(jnp.asarray(t) for t in tables))


def fits_kernel(n_row, n_col, source):
    row_cells, col_cells, z_cells = source.shape
    devices = n_row * n_col
    kept = (z_cells // 2) // devices
    blocks = n_col * kept
    return (
        kept * devices * 2 == z_cells
        and z_cells == 128
        and col_cells == 2 * SUBLANES
        and blocks * (col_cells // 2) == z_cells
        and blocks == row_cells // 2 + SWEEPS
        and row_cells >= 2 * SWEEPS
        and (row_cells + 2 * SWEEPS) % (SUBLANES // 2) == 0
    )


def solution(mesh):
    n_row, n_col = mesh.shape["row"], mesh.shape["col"]

    def local(source, coefficient):
        if fits_kernel(n_row, n_col, source):
            return local_kernel(n_row, n_col, source, coefficient)
        return local_general(source, coefficient)

    return jax.shard_map(
        local,
        mesh=mesh,
        in_specs=(P("row", "col", None), P("row", "col", None)),
        out_specs=P("row", "col", None),
        check_vma=False,
    )
```

```python
import jax
import jax.numpy as jnp
import numpy as np
from jax import lax
from jax.experimental import pallas as pl
from jax.experimental.pallas import tpu as pltpu
from jax.sharding import PartitionSpec as P

SWEEPS = 4


DAMPING = 0.8
SCREEN_SHIFT = 0.02
HIGHEST = lax.Precision.HIGHEST


def padded(block, sides, width):
    for axis, dim in sides:
        count = lax.axis_size(axis)
        forward = [(i, i + 1) for i in range(count - 1)]
        backward = [(target, source) for source, target in forward]
        low = lax.ppermute(
            lax.slice_in_dim(block, block.shape[dim] - width, None, axis=dim), axis, forward
        )
        high = lax.ppermute(lax.slice_in_dim(block, 0, width, axis=dim), axis, backward)
        block = jnp.concatenate([low, block, high], axis=dim)
    return block


def sine_table(length):
    series = jnp.arange(length, dtype=jnp.int32) + 1
    phases = series[:, None] * series[None, :] % (2 * (length + 1))
    return jnp.sin(jnp.pi * phases.astype(jnp.float32) / (length + 1))


def eigenvalues(positions, length):
    angles = jnp.pi * (positions + 1).astype(jnp.float32) / (2 * (length + 1))
    return 4.0 * jnp.sin(angles) ** 2


def neighbour_image(wide_field, diagonal_total):
    zpadded = jnp.pad(wide_field, ((0, 0), (0, 0), (1, 1)))
    center = wide_field[1:-1, 1:-1, :]
    beside = (
        wide_field[2:, 1:-1] + wide_field[:-2, 1:-1] + wide_field[1:-1, 2:] + wide_field[1:-1, :-2]
    )
    beside = beside + zpadded[1:-1, 1:-1, 2:] + zpadded[1:-1, 1:-1, :-2]
    return (center, diagonal_total * center - beside)


def relax_once(wide_field, diagonal_total, source):
    center, applied = neighbour_image(wide_field, diagonal_total)
    return center + DAMPING * (source - applied) / diagonal_total


def trim_rim(tensor, margin):
    return tensor[margin : tensor.shape[0] - margin, margin : tensor.shape[1] - margin]


def inside_table(row_cells, col_cells, margin):
    row_ids = (
        lax.axis_index("row") * row_cells
        - margin
        + jnp.arange(row_cells + 2 * margin, dtype=jnp.int32)
    )
    col_ids = (
        lax.axis_index("col") * col_cells
        - margin
        + jnp.arange(col_cells + 2 * margin, dtype=jnp.int32)
    )
    row_inside = (row_ids >= 0) & (row_ids < row_cells * lax.axis_size("row"))
    col_inside = (col_ids >= 0) & (col_ids < col_cells * lax.axis_size("col"))
    return (row_inside[:, None] & col_inside[None, :]).astype(jnp.float32)[:, :, None]


def coarse_solve(residual):
    row_cells, col_cells, z_cells = residual.shape
    coarse_rows = row_cells // 2
    coarse_cols = col_cells // 2
    coarse_z = z_cells // 2
    total_r = coarse_rows * lax.axis_size("row")
    total_c = coarse_cols * lax.axis_size("col")
    z_slab = coarse_z // lax.axis_size("row")
    r_slab = total_r // lax.axis_size("col")
    coarse = residual.reshape(coarse_rows, 2, coarse_cols, 2, coarse_z, 2).sum(axis=(1, 3, 5)) * 0.5
    table_z = sine_table(coarse_z)
    table_r = sine_table(total_r)
    table_c = sine_table(total_c)
    ordered = jnp.transpose(coarse, (2, 1, 0))
    along_z = jnp.dot(table_z, ordered.reshape(coarse_z, -1), precision=HIGHEST).reshape(
        coarse_z, coarse_cols, coarse_rows
    )
    row_lines = lax.all_to_all(along_z, "row", split_axis=0, concat_axis=2, tiled=True)
    along_r = jnp.einsum("zcr,kr->zkc", row_lines, table_r, precision=HIGHEST)
    col_lines = lax.all_to_all(along_r, "col", split_axis=1, concat_axis=2, tiled=True)
    spectrum = jnp.dot(col_lines.reshape(-1, total_c), table_c, precision=HIGHEST).reshape(
        z_slab, r_slab, total_c
    )
    normaliser = (coarse_z + 1.0) * (total_r + 1.0) * (total_c + 1.0) / 8.0
    lam_z = eigenvalues(
        lax.axis_index("row") * z_slab + jnp.arange(z_slab, dtype=jnp.int32), coarse_z
    )
    lam_r = eigenvalues(
        lax.axis_index("col") * r_slab + jnp.arange(r_slab, dtype=jnp.int32), total_r
    )
    lam_c = eigenvalues(jnp.arange(total_c, dtype=jnp.int32), total_c)
    denominator = (
        SCREEN_SHIFT + lam_z[:, None, None] + lam_r[None, :, None] + lam_c[None, None, :]
    ) * normaliser
    scaled = spectrum / denominator
    back_c = jnp.dot(scaled.reshape(-1, total_c), table_c, precision=HIGHEST).reshape(
        z_slab, r_slab, total_c
    )
    returned = lax.all_to_all(back_c, "col", split_axis=2, concat_axis=1, tiled=True)
    back_r = jnp.einsum("zkc,kr->zcr", returned, table_r, precision=HIGHEST)
    owned = lax.all_to_all(back_r, "row", split_axis=2, concat_axis=0, tiled=True)
    back_z = jnp.dot(table_z, owned.reshape(coarse_z, -1), precision=HIGHEST).reshape(
        coarse_z, coarse_cols, coarse_rows
    )
    correction = jnp.transpose(back_z, (2, 1, 0))
    return jnp.broadcast_to(
        correction[:, None, :, None, :, None], (coarse_rows, 2, coarse_cols, 2, coarse_z, 2)
    ).reshape(row_cells, col_cells, z_cells)


def local_general(source, coefficient):
    row_cells, col_cells, z_cells = source.shape
    diagonal_total = 6.0 + coefficient
    opening = DAMPING * source / diagonal_total
    wide_first, wide_source, wide_coef = (
        padded(opening, (("row", 0), ("col", 1)), SWEEPS),
        padded(source, (("row", 0), ("col", 1)), SWEEPS),
        padded(coefficient, (("row", 0), ("col", 1)), SWEEPS),
    )
    wide_diag = 6.0 + wide_coef
    inside = inside_table(row_cells, col_cells, SWEEPS)
    wide_iter = wide_first
    for repeat in range(1, SWEEPS):
        wide_iter = relax_once(
            wide_iter, trim_rim(wide_diag, repeat), trim_rim(wide_source, repeat)
        ) * trim_rim(inside, repeat)
    iterate, applied = neighbour_image(wide_iter, diagonal_total)
    residual = source - applied
    iterate = iterate + coarse_solve(residual)
    wide_iter = padded(iterate, (("row", 0), ("col", 1)), SWEEPS)
    for repeat in range(1, SWEEPS + 1):
        wide_iter = relax_once(
            wide_iter, trim_rim(wide_diag, repeat), trim_rim(wide_source, repeat)
        ) * trim_rim(inside, repeat)
    return wide_iter


MESH = pl.DeviceIdType.MESH
SUBLANES = 8
MOST_ROWS = 40


def plain_sine(length):
    series = np.arange(length) + 1
    phases = series[:, None] * series[None, :] % (2 * (length + 1))
    return np.sin(np.pi * phases / (length + 1))


def plain_eigen(length):
    return 4.0 * np.sin(np.pi * (np.arange(length) + 1) / (2 * (length + 1))) ** 2


def solve_tables(n_row, n_col, kept, coarse_rows, coarse_cols, coarse_z):
    blocks = n_col * kept
    total_r, total_c = n_row * coarse_rows, n_col * coarse_cols
    sine_z, sine_r, sine_c = plain_sine(coarse_z), plain_sine(total_r), plain_sine(total_c)
    table_z = np.repeat(sine_z, 2, axis=1)
    forward_r = np.zeros((total_r, n_row, blocks))
    forward_r[:, :, :coarse_rows] = sine_r.reshape(total_r, n_row, coarse_rows)
    window_r = np.zeros((n_row, blocks, total_r))
    margin = (blocks - coarse_rows) // 2
    for r in range(n_row):
        for a in range(blocks):
            at = coarse_rows * r - margin + a
            if 0 <= at < total_r:
                window_r[r, a] = sine_r[at]
    table_c = np.zeros((n_col, kept, coarse_cols, kept, total_c))
    for k in range(kept):
        table_c[:, k, :, k, :] = sine_c.reshape(n_col, coarse_cols, total_c)
    normaliser = (coarse_z + 1.0) * (total_r + 1.0) * (total_c + 1.0) / 8.0
    base = SCREEN_SHIFT + plain_eigen(total_r)[:, None] + np.tile(plain_eigen(total_c), kept)[None, :]
    lam_z = np.repeat(plain_eigen(coarse_z).reshape(n_row * n_col, 1, kept), total_c, axis=2)
    lanes = kept * total_c
    tables = (
        table_z,
        forward_r.reshape(total_r, n_row * blocks),
        window_r.reshape(n_row * blocks, total_r),
        table_c.reshape(lanes, lanes),
        base * 2.0 * normaliser,
        lam_z * 2.0 * normaliser,
    )
    return tuple(np.asarray(t, np.float32) for t in tables)


def block_transpose(x, width):
    rows, lanes = x.shape
    row = lax.broadcasted_iota(jnp.int32, x.shape, 0)
    group = lax.broadcasted_iota(jnp.int32, x.shape, 1) // width
    step = 1
    while step < rows:
        row_bit = (row & step) != 0
        group_bit = (group & step) != 0
        from_below = pltpu.roll(pltpu.roll(x, width * step, 1), rows - step, 0)
        from_above = pltpu.roll(pltpu.roll(x, lanes - width * step, 1), step, 0)
        x = jnp.where(row_bit == group_bit, x, jnp.where(group_bit, from_below, from_above))
        step *= 2
    return x


def split_dot(a, b, contract):
    def parts(x):
        high = x.astype(jnp.bfloat16)
        return high, (x - high.astype(jnp.float32)).astype(jnp.bfloat16)

    def product(x, y):
        return lax.dot_general(x, y, (contract, ((), ())), preferred_element_type=jnp.float32)

    (a_high, a_low), (b_high, b_low) = parts(a), parts(b)
    return product(a_high, b_high) + (product(a_high, b_low) + product(a_low, b_high))


def step_kernel(
    sizes,
    source,
    coefficient,
    table_z_in,
    forward_r_in,
    window_r_in,
    table_c_in,
    base_in,
    lam_z_in,
    out,
    table_z,
    forward_r,
    window_r,
    table_c,
    base,
    lam_z,
    wide_s,
    wide_c,
    weight,
    first,
    field_a,
    field_b,
    rows_sum,
    fine_corr,
    edge,
    send_a,
    recv_a,
    send_b,
    recv_b,
    own_sem,
    table_sem,
    halo_send,
    halo_recv,
    edge_send,
    edge_recv,
    fwd_send,
    fwd_recv,
    back_send,
    back_recv,
    ready,
):
    n_row, n_col, kept = sizes
    row_cells, col_cells, z_cells = source.shape
    coarse_rows, coarse_cols = row_cells // 2, col_cells // 2
    blocks = n_col * kept
    devices = n_row * n_col
    halo_r, halo_c = (wide_s.shape[0] - row_cells) // 2, SUBLANES
    wide_cols = wide_s.shape[1]
    my_row, my_col = lax.axis_index("row"), lax.axis_index("col")
    me = my_row * n_col + my_col

    steps = [(dr, dc) for dr in (-1, 0, 1) for dc in (-1, 0, 1) if (dr, dc) != (0, 0)]

    def exists(dr, dc):
        r, c = my_row + dr, my_col + dc
        return (r >= 0) & (r < n_row) & (c >= 0) & (c < n_col)

    barrier = pltpu.get_barrier_semaphore()
    for d in range(1, n_row):
        pl.semaphore_signal(
            barrier, 1, device_id=(lax.rem(my_row + d, n_row), my_col), device_id_type=MESH
        )
    for d in range(1, n_col):
        pl.semaphore_signal(
            barrier, 1, device_id=(my_row, lax.rem(my_col + d, n_col)), device_id_type=MESH
        )
    greeted = n_row + n_col - 2
    for dr, dc in steps:
        if dr and dc:
            there = exists(dr, dc)

            @pl.when(there)
            def _():
                pl.semaphore_signal(
                    barrier, 1, device_id=(my_row + dr, my_col + dc), device_id_type=MESH
                )

            greeted = greeted + there.astype(jnp.int32)

    arrays = ((source, wide_s), (coefficient, wide_c))
    own = [
        pltpu.make_async_copy(
            here, wide.at[pl.ds(halo_r, row_cells), pl.ds(0, col_cells)], own_sem.at[n]
        )
        for n, (here, wide) in enumerate(arrays)
    ]
    for copy in own:
        copy.start()
    staged = [
        pltpu.make_async_copy(given, held, table_sem.at[n])
        for n, (given, held) in enumerate(
            (
                (table_z_in, table_z),
                (forward_r_in, forward_r),
                (window_r_in, window_r),
                (table_c_in, table_c),
                (base_in, base),
                (lam_z_in, lam_z),
            )
        )
    ]
    for copy in staged:
        copy.start()

    def landing(dr, dc):
        rows = {-1: (0, halo_r), 0: (halo_r, row_cells), 1: (halo_r + row_cells, halo_r)}[dr]
        cols = {
            -1: (col_cells + halo_c, halo_c),
            0: (0, col_cells),
            1: (col_cells, halo_c),
        }[dc]
        return pl.ds(*rows), pl.ds(*cols)

    def leaving(dr, dc):
        rows = {-1: (0, halo_r), 0: (0, row_cells), 1: (row_cells - halo_r, halo_r)}[dr]
        cols = {-1: (0, halo_c), 0: (0, col_cells), 1: (col_cells - halo_c, halo_c)}[dc]
        return pl.ds(*rows), pl.ds(*cols)

    def halo_copies(dr, dc):
        at = steps.index((dr, dc))
        return [
            pltpu.make_async_remote_copy(
                src_ref=here.at[leaving(dr, dc)],
                dst_ref=wide.at[landing(-dr, -dc)],
                send_sem=halo_send.at[n, at],
                recv_sem=halo_recv.at[n, at],
                device_id=(my_row + dr, my_col + dc),
                device_id_type=MESH,
            )
            for n, (here, wide) in enumerate(arrays)
        ]

    pl.semaphore_wait(barrier, greeted)
    for step in steps:

        @pl.when(exists(*step))
        def _():
            for copy in halo_copies(*step):
                copy.start()

    for d in range(1, n_row):
        pl.semaphore_signal(
            ready, 1, device_id=(lax.rem(my_row + d, n_row), my_col), device_id_type=MESH
        )
    for step in steps:

        @pl.when(jnp.logical_not(exists(*step)))
        def _():
            rows, cols = landing(*step)
            for _, wide in arrays:
                wide[rows, cols] = jnp.zeros((rows.size, cols.size, z_cells), jnp.float32)

    for copy in own:
        copy.wait()
    for dr, dc in steps:
        @pl.when(exists(-dr, -dc))
        def _():
            for copy in halo_copies(dr, dc):
                copy.wait_recv()

    wide_rows = wide_s.shape[0]
    col_at = lax.broadcasted_iota(jnp.int32, (wide_cols, z_cells), 0)
    z_at = lax.broadcasted_iota(jnp.int32, (wide_cols, z_cells), 1)
    col_at = my_col * col_cells + jnp.where(col_at >= col_cells + halo_c, col_at - wide_cols, col_at)
    col_inside = (col_at >= 0) & (col_at < n_col * col_cells)
    not_first = z_at > 0
    not_last = z_at < z_cells - 1

    def prepare(i):
        at = my_row * row_cells + i - halo_r
        inside = (at >= 0) & (at < n_row * row_cells)
        scale = jnp.where(inside & col_inside, DAMPING / (6.0 + wide_c[i]), 0.0)
        weight[i] = scale
        first[i] = scale * wide_s[i]

    piece = SUBLANES // 2

    @pl.loop(0, wide_rows // piece)
    def _(n):
        for m in range(piece):
            prepare(n * piece + m)

    def beside(above, here, below):
        cols = here.shape[0]
        low = jnp.where(not_first[:cols], pltpu.roll(here, 1, 1), 0.0)
        high = jnp.where(not_last[:cols], pltpu.roll(here, z_cells - 1, 1), 0.0)
        return (
            (above + below)
            + (pltpu.roll(here, 1, 0) + pltpu.roll(here, cols - 1, 0))
            + (low + high)
        )

    def sweep(old, new, low, high, shift=0, cols=wide_cols):
        chunk = max(m for m in range(1, MOST_ROWS + 1) if (high - low) % m == 0)

        def work(i):
            lines = [old[i - 1 + m] for m in range(chunk + 2)]
            for m in range(chunk):
                here = lines[m + 1]
                fresh = (1.0 - DAMPING) * here + (
                    first[i + m] + weight[i + m] * beside(lines[m], here, lines[m + 2])
                )
                new[i + m - shift] = fresh[:cols]

        if chunk == high - low:
            work(low)
        else:

            @pl.loop(0, (high - low) // chunk)
            def _(n):
                work(low + n * chunk)

    fields = (first,) + (field_b, field_a) * SWEEPS
    smooth, other = fields[SWEEPS - 1], fields[SWEEPS]
    for turn in range(1, SWEEPS):
        sweep(fields[turn - 1], fields[turn], turn, wide_rows - turn)

    edge_rows = halo_r - 1
    edge_at = (0, halo_r + row_cells + 1)

    def edge_copy(dr):
        return pltpu.make_async_remote_copy(
            src_ref=smooth.at[
                pl.ds(halo_r + (1 if dr < 0 else row_cells - halo_r), edge_rows)
            ],
            dst_ref=edge.at[1 if dr < 0 else 0],
            send_sem=edge_send.at[1 if dr < 0 else 0],
            recv_sem=edge_recv.at[1 if dr < 0 else 0],
            device_id=(my_row + dr, my_col),
            device_id_type=MESH,
        )

    def start_edges():
        for dr in (-1, 1):

            @pl.when(exists(dr, 0))
            def _():
                edge_copy(dr).start()

    @pl.loop(0, coarse_rows)
    def _(a):
        i = halo_r + 2 * a
        lines = [smooth[i - 1 + m] for m in range(4)]
        total = None
        for m in range(2):
            near = beside(lines[m], lines[m + 1], lines[m + 2])
            left = wide_s[i + m] + (near - (6.0 + wide_c[i + m]) * lines[m + 1])
            total = left if total is None else total + left
        rows_sum[a] = total[:col_cells]

    for copy in staged:
        copy.wait()
    pairs = [
        rows_sum[a, pl.ds(0, coarse_cols, stride=2), :]
        + rows_sum[a, pl.ds(1, coarse_cols, stride=2), :]
        for a in range(coarse_rows)
    ]
    blank = jnp.zeros(((blocks - coarse_rows) * coarse_cols, z_cells), jnp.float32)
    along_z = split_dot(
        table_z[...], jnp.concatenate(pairs + [blank], axis=0), ((1,), (1,))
    )
    for q in range(devices):
        send_a[q] = along_z[q * kept : (q + 1) * kept]

    pl.semaphore_wait(ready, n_row - 1)

    def exchange(send, recv, send_sem, recv_sem, meanwhile=None):
        def copy(d):
            target = lax.rem(me + d, devices)
            return pltpu.make_async_remote_copy(
                src_ref=send.at[target],
                dst_ref=recv.at[me],
                send_sem=send_sem.at[d],
                recv_sem=recv_sem.at[d],
                device_id=(lax.div(target, n_col), lax.rem(target, n_col)),
                device_id_type=MESH,
            )

        @pl.loop(1, devices, unroll=True)
        def _(d):
            copy(d).start()

        recv[me] = send[me]
        if meanwhile is not None:
            meanwhile()

        @pl.loop(1, devices, unroll=True)
        def _(d):
            copy(d).wait_send()

        @pl.loop(1, devices, unroll=True)
        def _(d):
            copy(d).wait_recv()

    exchange(send_a, recv_a, fwd_send, fwd_recv, start_edges)

    gathered = jnp.concatenate(
        [
            block_transpose(
                recv_a[pl.ds(r * n_col, n_col)].reshape(blocks, z_cells), coarse_cols
            )
            for r in range(n_row)
        ],
        axis=0,
    )
    along_r = split_dot(forward_r[...], gathered, ((1,), (0,)))
    spectrum = split_dot(along_r, table_c[...], ((1,), (0,)))
    scaled = spectrum / (base[...] + lam_z[me])
    back_c = split_dot(scaled, table_c[...], ((1,), (1,)))
    back_r = split_dot(window_r[...], back_c, ((1,), (0,)))
    lane = lax.broadcasted_iota(jnp.int32, (blocks, z_cells), 1)
    column = lane // (kept * coarse_cols)
    late = lane % coarse_cols >= coarse_cols // 2
    for r in range(n_row):
        plane = back_r[r * blocks : (r + 1) * blocks]
        right = jnp.where(
            column < n_col - 1, pltpu.roll(plane, z_cells - kept * coarse_cols, 1), 0.0
        )
        left = jnp.where(column > 0, pltpu.roll(plane, kept * coarse_cols, 1), 0.0)
        at = pl.ds(r * n_col, n_col)
        send_b[at, pl.ds(0, kept)] = block_transpose(plane, coarse_cols).reshape(
            n_col, kept, z_cells
        )
        send_b[at, pl.ds(kept, kept)] = block_transpose(
            jnp.where(late, left, right), coarse_cols
        ).reshape(n_col, kept, z_cells)

    def end_halo():
        for step in steps:

            @pl.when(exists(*step))
            def _():
                for copy in halo_copies(*step):
                    copy.wait_send()

    exchange(send_b, recv_b, back_send, back_recv, end_halo)

    modes = devices * kept
    for part in range(2):
        lines = recv_b[:, pl.ds(part * kept, kept)].reshape(modes, z_cells)
        values = split_dot(jnp.transpose(lines), table_z[...], ((1,), (0,)))
        for a in range(blocks):
            for odd in range(2):
                fine_corr[a, pl.ds(part * col_cells + odd, coarse_cols, stride=2), :] = values[
                    a * coarse_cols : (a + 1) * coarse_cols
                ]

    for dr in (-1, 1):
        slot = 1 if dr < 0 else 0

        @pl.when(exists(dr, 0))
        def _():
            edge_copy(dr).wait_send()

        @pl.when(exists(-dr, 0))
        def _():
            edge_copy(dr).wait_recv()
            smooth[pl.ds(edge_at[slot], edge_rows)] = edge[slot]

        @pl.when(jnp.logical_not(exists(-dr, 0)))
        def _():
            smooth[pl.ds(edge_at[slot], edge_rows)] = jnp.zeros(edge.shape[1:], jnp.float32)

    margin = halo_r - (blocks - coarse_rows)

    @pl.loop(0, blocks)
    def _(a):
        i = margin + 2 * a
        smooth[i] = smooth[i] + fine_corr[a]
        smooth[i + 1] = smooth[i + 1] + fine_corr[a]

    fields = (smooth, other) * SWEEPS
    for turn in range(SWEEPS):
        low, high = margin + 1 + turn, wide_rows - margin - 1 - turn
        if turn < SWEEPS - 1:
            sweep(fields[turn], fields[turn + 1], low, high)
        else:
            sweep(fields[turn], out, low, high, low, col_cells)


def local_kernel(n_row, n_col, source, coefficient):
    row_cells, col_cells, z_cells = source.shape
    coarse_rows, coarse_cols, coarse_z = row_cells // 2, col_cells // 2, z_cells // 2
    devices = n_row * n_col
    kept = coarse_z // devices
    blocks = n_col * kept
    tables = solve_tables(n_row, n_col, kept, coarse_rows, coarse_cols, coarse_z)
    wide = (row_cells + 2 * SWEEPS, col_cells + 2 * SUBLANES, z_cells)
    dma = pltpu.SemaphoreType.DMA
    f32 = jnp.float32

    def body(*refs):
        step_kernel((n_row, n_col, kept), *refs)

    return pl.pallas_call(
        body,
        out_shape=jax.ShapeDtypeStruct(source.shape, f32),
        in_specs=[pl.BlockSpec(memory_space=pl.ANY)] * (2 + len(tables)),
        out_specs=pl.BlockSpec(memory_space=pltpu.VMEM),
        scratch_shapes=[pltpu.VMEM(t.shape, f32) for t in tables]
        + [pltpu.VMEM(wide, f32)] * 6
        + [
            pltpu.VMEM((coarse_rows, col_cells, z_cells), f32),
            pltpu.VMEM((blocks, 2 * col_cells, z_cells), f32),
            pltpu.VMEM((2, SWEEPS - 1) + wide[1:], f32),
            pltpu.VMEM((devices, kept, z_cells), f32),
            pltpu.VMEM((devices, kept, z_cells), f32),
            pltpu.VMEM((devices, 2 * kept, z_cells), f32),
            pltpu.VMEM((devices, 2 * kept, z_cells), f32),
            dma((2,)),
            dma((len(tables),)),
            dma((2, 8)),
            dma((2, 8)),
            dma((2,)),
            dma((2,)),
            dma((devices,)),
            dma((devices,)),
            dma((devices,)),
            dma((devices,)),
            pltpu.SemaphoreType.REGULAR,
        ],
        compiler_params=pltpu.CompilerParams(collective_id=0, has_side_effects=True),
        name="vstep",
    )(source, coefficient, *(jnp.asarray(t) for t in tables))


def fits_kernel(n_row, n_col, source):
    row_cells, col_cells, z_cells = source.shape
    devices = n_row * n_col
    kept = (z_cells // 2) // devices
    blocks = n_col * kept
    return (
        kept * devices * 2 == z_cells
        and z_cells == 128
        and col_cells == 2 * SUBLANES
        and blocks * (col_cells // 2) == z_cells
        and blocks == row_cells // 2 + SWEEPS
        and row_cells >= 2 * SWEEPS
        and (row_cells + 2 * SWEEPS) % (SUBLANES // 2) == 0
    )


def solution(mesh):
    n_row, n_col = mesh.shape["row"], mesh.shape["col"]

    def local(source, coefficient):
        if fits_kernel(n_row, n_col, source):
            return local_kernel(n_row, n_col, source, coefficient)
        return local_general(source, coefficient)

    return jax.shard_map(
        local,
        mesh=mesh,
        in_specs=(P("row", "col", None), P("row", "col", None)),
        out_specs=P("row", "col", None),
        check_vma=False,
    )
```
